256 devices in a mesh: pb: 32 (over y, z_lo, core), ka: 8 (over z_hi, x).
Axes of the slice: x: 4, y: 4, z: 8 (z_hi: 2, z_lo: 4; z = z_hi * 4 + z_lo), core: 2. Of those that a mesh axis runs over, the one named last changes fastest.
Arguments:
- queries: bfloat16 [32768, 1024], P(('pb', 'ka')), may hold values from -6 to 6
- key_vectors: bfloat16 [32768, 128], P(('pb', 'ka')), may hold values from -6 to 6
- value_vectors: bfloat16 [32768, 128], P(('pb', 'ka')), may hold values from -6 to 6
- out_grad: bfloat16 [32768, 1024], P(('pb', 'ka')), may hold values from -6 to 6
- rand_blocks: int32 [512, 3], P('pb'), may hold values from 0 to 511
- global_blocks: int32 [2], replicated, may hold values from 0 to 511
Outputs:
- attended: bfloat16 [32768, 1024], P(('pb', 'ka'))
- query_grad: bfloat16 [32768, 1024], P(('pb', 'ka'))
- key_grad: bfloat16 [32768, 128], P(('pb', 'ka'))
- value_grad: bfloat16 [32768, 128], P(('pb', 'ka'))
The draws below stay inside these ranges and needn't reach their ends.
All inputs are finite; a program needn't handle non-finite values.
Results may differ from the reference program's by a relative error of at most 0.024.
Values may be sent and summed in bfloat16 or wider, within the bound.
A program may use at most 128 MiB of HBM per device.

```python
import math
import jax
import jax.numpy as jnp
from jax import lax

HEAD_DIM = 128
HEADS = 8
BLOCK = 64
GLOB = 2
RAND = 3
SEQ = 32768
NBLK = 512


def pair_draw(key):
    q_key = jax.random.fold_in(key, 11)
    k_key = jax.random.fold_in(key, 12)
    full_width = HEADS * HEAD_DIM
    query_vals = jnp.clip(jax.random.normal(q_key, (SEQ, full_width), jnp.float32), -5.0, 5.0)
    key_vals = jnp.clip(jax.random.normal(k_key, (SEQ, HEAD_DIM), jnp.float32), -5.0, 5.0)
    return (query_vals.astype(jnp.bfloat16), key_vals.astype(jnp.bfloat16))


def draw_queries(key, part):
    return pair_draw(key)[0]


def draw_key_vectors(key, part):
    return pair_draw(key)[1]


def with_ends(drawn, stream_key, low, top_value):
    longest = drawn.shape.index(max(drawn.shape))
    spots = []
    for shift in (0, 1):
        where = [jax.random.randint(jax.random.fold_in(stream_key, axis), (), 0, length) for axis, length in enumerate(drawn.shape)]
        where[longest] = (where[longest] + shift) % drawn.shape[longest]
        spots.append(tuple(where))
    return drawn.at[spots[0]].set(low).at[spots[1]].set(top_value)


def steps_of(stream_key, extent, cuts, least, largest):
    loudness, own = 1.0, jax.random.fold_in(stream_key, 6)
    for dim, blocks in cuts:
        steps = jnp.exp(jax.random.uniform(jax.random.fold_in(own, dim), (blocks,), jnp.float32, least / len(cuts), largest / len(cuts)))
        loudness = loudness * jnp.repeat(steps, extent[dim] // blocks).reshape([-1 if axis == dim else 1 for axis in range(len(extent))])
    return loudness


def noise(key, extent, width, most, pieces=(), held_as=jnp.bfloat16):
    values = width * jax.random.normal(key, extent, jnp.float32)
    if pieces:
        values = values * steps_of(key, extent, pieces, -0.22, 0.18)
    return jnp.clip(values, -most, most).astype(held_as)


def setup_inputs(seed: int = 0) -> dict:
    keys = jax.random.split(jax.random.key(seed), 7)
    queries = draw_queries(jax.random.fold_in(keys[6], 71), 0)
    key_vectors = draw_key_vectors(jax.random.fold_in(keys[6], 71), 0)
    value_vectors = noise(keys[2], (SEQ, HEAD_DIM), 1.0, 6.0, ((0, 256),))
    out_grad = noise(keys[3], (SEQ, HEADS * HEAD_DIM), 1.0, 6.0, ((0, 256),))
    rand_blocks = with_ends(jax.random.randint(keys[4], (NBLK, RAND), 0, NBLK), jax.random.fold_in(keys[4], 1), 0, NBLK - 1).astype(jnp.int32)
    global_blocks = jax.random.randint(keys[5], (GLOB,), 0, NBLK).astype(jnp.int32)
    return dict(queries=queries, key_vectors=key_vectors, value_vectors=value_vectors, out_grad=out_grad, rand_blocks=rand_blocks, global_blocks=global_blocks)


NEG_FILL = -1e+30

def candidates(block_ids, global_blocks, rand_rows, block_total):
    nearby = jnp.stack([block_ids - 1, block_ids, block_ids + 1], axis=1)
    global_cols = jnp.broadcast_to(global_blocks[None, :], (block_ids.shape[0], global_blocks.shape[0]))
    cand = jnp.concatenate([nearby, global_cols, rand_rows], axis=1).astype(jnp.int32)
    in_range = (cand >= 0) & (cand < block_total)
    slot_count = cand.shape[1]
    equal_pairs = cand[:, :, None] == cand[:, None, :]
    earlier_slot = jnp.arange(slot_count)[None, :, None] > jnp.arange(slot_count)[None, None, :]
    repeated = jnp.any(equal_pairs & earlier_slot, axis=2)
    valid_slots = in_range & jnp.logical_not(repeated)
    safe_slots = jnp.clip(cand, 0, block_total - 1).astype(jnp.int32)
    return (safe_slots, valid_slots)

def reference(queries, key_vectors, value_vectors, out_grad, rand_blocks, global_blocks):
    block_total = SEQ // BLOCK
    score_scale = 1.0 / math.sqrt(HEAD_DIM)
    block_ids = jnp.arange(block_total, dtype=jnp.int32)
    safe_slots, valid_slots = candidates(block_ids, global_blocks, rand_blocks, block_total)
    slot_count = safe_slots.shape[1]
    is_global = jnp.any(block_ids[:, None] == global_blocks[None, :], axis=1)
    q_blocks = queries.reshape(block_total, BLOCK * HEADS, HEAD_DIM)
    d_blocks = out_grad.reshape(block_total, BLOCK * HEADS, HEAD_DIM)
    k_blocks = key_vectors.reshape(block_total, BLOCK, HEAD_DIM)
    v_blocks = value_vectors.reshape(block_total, BLOCK, HEAD_DIM)

    def sparse_weights(block_id):
        picked = k_blocks[safe_slots[block_id]].reshape(slot_count * BLOCK, HEAD_DIM)
        picked_vals = v_blocks[safe_slots[block_id]].reshape(slot_count * BLOCK, HEAD_DIM)
        key_mask = jnp.repeat(valid_slots[block_id], BLOCK)[None, :]
        raw_scores = jnp.dot(q_blocks[block_id], picked.T, preferred_element_type=jnp.float32) * score_scale
        row_max = lax.optimization_barrier(jnp.max(jnp.where(key_mask, raw_scores, NEG_FILL), axis=1, keepdims=True))
        expo_terms = jnp.where(key_mask, jnp.exp(raw_scores - row_max), 0.0)
        row_sum = lax.optimization_barrier(jnp.sum(expo_terms, axis=1, keepdims=True))
        weights = expo_terms / row_sum * jnp.where(is_global[block_id], 0.0, 1.0)
        return (weights, picked, picked_vals)

    def forward_block(block_id):
        weights, picked, picked_vals = sparse_weights(block_id)
        return jnp.dot(weights.astype(jnp.bfloat16), picked_vals, preferred_element_type=jnp.float32)
    out_blocks = lax.map(forward_block, block_ids)

    def dense_weights(block_id):
        raw_scores = jnp.dot(q_blocks[block_id], key_vectors.T, preferred_element_type=jnp.float32) * score_scale
        row_max = lax.optimization_barrier(jnp.max(raw_scores, axis=1, keepdims=True))
        expo_terms = jnp.exp(raw_scores - row_max)
        return expo_terms / lax.optimization_barrier(jnp.sum(expo_terms, axis=1, keepdims=True))
    for global_slot in range(GLOB):
        block_id = global_blocks[global_slot]
        weights = dense_weights(block_id)
        partial_value = jnp.dot(weights.astype(jnp.bfloat16), value_vectors, preferred_element_type=jnp.float32)
        out_blocks = out_blocks.at[block_id].set(partial_value)
    attended = out_blocks.reshape(SEQ, HEADS * HEAD_DIM).astype(jnp.bfloat16)
    row_dot = lax.optimization_barrier(jnp.sum((out_grad.astype(jnp.float32) * attended.astype(jnp.float32)).reshape(block_total, BLOCK * HEADS, HEAD_DIM), axis=2))

    def backward_block(carry_in, block_id):
        key_acc, value_acc = carry_in
        weights, picked, picked_vals = sparse_weights(block_id)
        weights_bf = weights.astype(jnp.bfloat16)
        prob_grad = jnp.dot(d_blocks[block_id], picked_vals.T, preferred_element_type=jnp.float32)
        score_grad = (weights * (prob_grad - row_dot[block_id][:, None])).astype(jnp.bfloat16)
        query_part = jnp.dot(score_grad, picked, preferred_element_type=jnp.float32) * score_scale
        key_part = (jnp.dot(score_grad.T, q_blocks[block_id], preferred_element_type=jnp.float32) * score_scale).reshape(slot_count, BLOCK, HEAD_DIM)
        value_part = jnp.dot(weights_bf.T, d_blocks[block_id], preferred_element_type=jnp.float32).reshape(slot_count, BLOCK, HEAD_DIM)
        key_acc = key_acc.at[safe_slots[block_id]].add(key_part)
        value_acc = value_acc.at[safe_slots[block_id]].add(value_part)
        return ((key_acc, value_acc), query_part)
    zero_keys = jnp.zeros((block_total, BLOCK, HEAD_DIM), jnp.float32)
    (key_acc, value_acc), dq_blocks = lax.scan(backward_block, (zero_keys, zero_keys), block_ids)
    for global_slot in range(GLOB):
        block_id = global_blocks[global_slot]
        first_use = jnp.where(jnp.any(global_blocks[:global_slot] == block_id), 0.0, 1.0)
        weights = dense_weights(block_id)
        weights_bf = weights.astype(jnp.bfloat16)
        prob_grad = jnp.dot(d_blocks[block_id], value_vectors.T, preferred_element_type=jnp.float32)
        score_grad = (weights * (prob_grad - row_dot[block_id][:, None])).astype(jnp.bfloat16)
        dq_blocks = dq_blocks.at[block_id].set(jnp.dot(score_grad, key_vectors, preferred_element_type=jnp.float32) * score_scale)
        key_acc = key_acc + first_use * (jnp.dot(score_grad.T, q_blocks[block_id], preferred_element_type=jnp.float32) * score_scale).reshape(block_total, BLOCK, HEAD_DIM)
        value_acc = value_acc + first_use * jnp.dot(weights_bf.T, d_blocks[block_id], preferred_element_type=jnp.float32).reshape(block_total, BLOCK, HEAD_DIM)
    query_grad = dq_blocks.reshape(SEQ, HEADS * HEAD_DIM).astype(jnp.bfloat16)
    key_grad = key_acc.reshape(SEQ, HEAD_DIM).astype(jnp.bfloat16)
    value_grad = value_acc.reshape(SEQ, HEAD_DIM).astype(jnp.bfloat16)
    return (attended, query_grad, key_grad, value_grad)
```

```python
import math

import jax
import jax.numpy as jnp
from jax import lax
from jax.experimental import pallas as pl
from jax.experimental.pallas import tpu as pltpu
from jax.sharding import PartitionSpec as P

NX, NY, NZ = 4, 4, 8
PLANE = NY * NZ
SHARDS = 256
NBLK = 512
BLOCK = 64
HD = 128
HEADS = 8
SLOTS = 8
SCALE = 1.0 / math.sqrt(HD)
NEG = -1e30
MESH = pl.DeviceIdType.MESH
F32, BF16 = jnp.float32, jnp.bfloat16


def here():
    pb, ka = lax.axis_index("pb"), lax.axis_index("ka")
    return ka % 4, pb // 8, (ka // 4) * 4 + (pb // 2) % 4, pb % 2


def device(x, y, z, c):
    return ((y * 4 + z % 4) * 2 + c, (z // 4) * 4 + x)


def place(block):
    shard = block // 2
    pb, ka = shard // 8, shard % 8
    return ka % 4, pb % 2, (pb // 8) * 8 + (ka // 4) * 4 + (pb // 2) % 4, block % 2


def remote(src, dst, ssem, rsem, dev):
    return pltpu.make_async_remote_copy(
        src_ref=src, dst_ref=dst, send_sem=ssem, recv_sem=rsem, device_id=dev, device_id_type=MESH
    )


def ring_steps(n):
    last = n // 2 - 1
    return [(d, k, k == last) for k in range(last + 1) for d in (0, 1)]


def gather_flow(piece, half, order, pos, core, sems, arrived):
    x, y, z = pos
    ssem, rsem = sems
    size = {"y": NY, "z": NZ}
    n1, n2 = size[order[0]], size[order[1]]

    def at(o1, o2):
        oy, oz = (o1, o2) if order[0] == "y" else (o2, o1)
        return (y + oy + NY) % NY, (z + oz + NZ) % NZ

    def dev(axis, step):
        if axis == "y":
            return device(x, (y + step + NY) % NY, z, core)
        return device(x, y, (z + step + NZ) % NZ, core)

    def ref(o1, o2, d, halved):
        cy, cz = at(o1, o2)
        return half(cy, cz, d) if halved else piece(cy, cz)

    def copy(o1, o2, d, halved, axis, sem):
        r = ref(o1, o2, d, halved)
        return remote(r, r, ssem.at[sem], rsem.at[sem], dev(axis, 1 if d == 0 else -1))

    offsets = [0]
    for k in range(1, n1 // 2):
        offsets += [-k, k]
    offsets.append(n1 // 2)
    ready = {o: abs(o) for o in offsets}
    plan = {}

    def add(r, what):
        plan.setdefault(r, []).append(what)

    for d, k, halved in ring_steps(n1):
        sign = -1 if d == 0 else 1
        add(k, ("send", sign * k, 0, d, halved, order[0], d * (n1 // 2) + k))
        add(k + 1, ("wait", sign * (k + 1), 0, d, halved, order[0], d * (n1 // 2) + k))
    for i, o in enumerate(offsets):
        for d, k, halved in ring_steps(n2):
            sign = -1 if d == 0 else 1
            sem = n1 + i * n2 + d * (n2 // 2) + k
            add(ready[o] + k, ("send", o, sign * k, d, halved, order[1], sem))
            add(ready[o] + k + 1, ("wait", o, sign * (k + 1), d, halved, order[1], sem))
    sends = []
    for r in range(max(plan) + 1):
        full = set()
        for what, o1, o2, d, halved, axis, sem in plan[r]:
            if what == "wait":
                copy(o1, o2, d, halved, axis, sem).wait_recv()
                if not halved or d == 1:
                    full.add((o1, o2))
        for o1, o2 in sorted(full):
            arrived(*at(o1, o2))
        for what, o1, o2, d, halved, axis, sem in plan[r]:
            if what == "send":
                cp = copy(o1, o2, d, halved, axis, sem)
                cp.start()
                sends.append(cp)
        yield
    for cp in sends:
        cp.wait_send()


GATHER_SEMS = {("y", "z"): NY + NY * NZ, ("z", "y"): NZ + NZ * NY}


def reduce_flow(own, got, out, order, pos, core, sems, done):
    x, y, z = pos
    ssem, rsem = sems
    size = {"y": NY, "z": NZ}
    n1, n2 = size[order[0]], size[order[1]]
    rows = HD // 2

    def at(o1, o2):
        oy, oz = (o1, o2) if order[0] == "y" else (o2, o1)
        return (y + oy + NY) % NY, (z + oz + NZ) % NZ

    def dev(axis, step):
        if axis == "y":
            return device(x, (y + step + NY) % NY, z, core)
        return device(x, y, (z + step + NZ) % NZ, core)

    def copy(src, i, halved, d, axis):
        dst = got.at[i]
        if halved:
            dst = dst.at[pl.ds(d * rows, rows)]
        return remote(src, dst, ssem.at[i], rsem.at[i], dev(axis, 1 if d == 0 else -1))

    def half_of(ref, d):
        return ref.at[pl.ds(d * rows, rows)]

    offsets = [n2 // 2]
    for k in range(n2 // 2 - 1, 0, -1):
        offsets += [-k, k]
    offsets.append(0)
    start = {o: n2 // 2 - abs(o) for o in offsets}
    plan = {}

    def add(r, kind, fn):
        plan.setdefault(r, {}).setdefault(kind, []).append(fn)

    sends = []

    def ring(n, axis, base, r0, term, result):
        steps = n // 2
        for d in (0, 1):
            sign = 1 if d == 0 else -1
            for t in range(steps):
                i = base + d * steps + t
                o = sign * (steps - t)

                def send(i=i, o=o, t=t, d=d):
                    ref, value = term(o)
                    if t == 0:
                        if ref is None:
                            half_of(out.at[i], d)[...] = value(d).astype(BF16)
                            src = half_of(out.at[i], d)
                        else:
                            src = half_of(ref, d)
                        cp = copy(src, i, True, d, axis)
                    else:
                        if t == 1:
                            got_half = half_of(got.at[i - 1], d)[...].astype(F32)
                            half_of(out.at[i], d)[...] = (value(d) + got_half).astype(BF16)
                            half_of(out.at[i], 1 - d)[...] = value(1 - d).astype(BF16)
                        else:
                            out[i] = (value(None) + got[i - 1].astype(F32)).astype(BF16)
                        cp = copy(out.at[i], i, False, d, axis)
                    cp.start()
                    sends.append(cp)

                def wait(i=i, t=t, d=d):
                    src = half_of(out.at[i], d) if t == 0 else out.at[i]
                    copy(src, i, t == 0, d, axis).wait_recv()

                add(r0 + t, "send", send)
                add(r0 + t + 1, "wait", wait)
        result(r0 + steps, base)

    s1, s2 = n1 // 2, n2 // 2
    for j, o2 in enumerate(offsets):

        def term(o1, o2=o2):
            r = own(*at(o1, o2))

            def value(h, r=r):
                return (r[...] if h is None else half_of(r, h)[...]).astype(F32)

            return r, value

        ring(n1, order[0], j * n1, start[o2], term, lambda r, base: None)

    def term2(o2):
        base = offsets.index(abs(o2) if abs(o2) == n2 // 2 else o2) * n1
        a, b = base + s1 - 1, base + n1 - 1

        def value(h):
            r = own(*at(0, o2))
            if h is None:
                return r[...].astype(F32) + got[a].astype(F32) + got[b].astype(F32)
            return (
                half_of(r, h)[...].astype(F32)
                + half_of(got.at[a], h)[...].astype(F32)
                + half_of(got.at[b], h)[...].astype(F32)
            )

        return None, value

    base2 = n1 * n2
    ring(n2, order[1], base2, start[n2 // 2] + s1, term2, lambda r, base: None)
    for r in range(max(plan) + 1):
        for fn in plan[r].get("wait", []):
            fn()
        for fn in plan[r].get("send", []):
            fn()
        yield
    value = term2(0)[1](None)
    value += got[base2 + s2 - 1].astype(F32) + got[base2 + n2 - 1].astype(F32)
    done(value)
    for cp in sends:
        cp.wait_send()


REDUCE_MSGS = {("y", "z"): NY * NZ + NZ, ("z", "y"): NZ * NY + NY}


def run_rounds(*flows):
    flows = list(flows)
    while flows:
        alive = []
        for f in flows:
            try:
                next(f)
                alive.append(f)
            except StopIteration:
                pass
        flows = alive


def greet(devices):
    barrier = pltpu.get_barrier_semaphore()
    for dev in devices:
        pl.semaphore_signal(barrier, inc=1, device_id=dev, device_id_type=MESH)
    pl.semaphore_wait(barrier, len(devices))


def nt(a, b):
    return lax.dot_general(a, b, (((1,), (1,)), ((), ())), preferred_element_type=F32)


def tn(a, b):
    return lax.dot_general(a, b, (((0,), (0,)), ((), ())), preferred_element_type=F32)


def nn(a, b):
    return lax.dot_general(a, b, (((1,), (0,)), ((), ())), preferred_element_type=F32)


def kernel_a(
    rand, glob, rand_any, q, k, v, d,
    att, dq, contrib, gp, gs, gq, gd, near_sum, gout, rand_sib,
    col, gch, sel, xbuf, xsend, near, near_send, near_got, cbuf, stat, part,
    sg, dpg, kc, vc, qs, ds_, dkv, own_sum,
    a_ssem, a_rsem, b_ssem, b_rsem, c_ssem, c_rsem, ssem, rsem, lsem,
):
    x, y, z, c = here()
    pb, ka = lax.axis_index("pb"), lax.axis_index("ka")
    shard = pb * 8 + ka
    me = y * NZ + z
    row = c * 4 + x
    zh = z // 4

    def plane_dev(p):
        return device(x, p // NZ, p % NZ, c)

    def row_dev(r):
        return device(r % 4, y, z, r // 4)

    def shard_dev(s):
        return (s // 8, s % 8)

    nxt, prv = (shard + 1) % SHARDS, (shard + SHARDS - 1) % SHARDS
    row_peers = [(row + i) % 8 for i in range(1, 8)]
    x_peers = [c * 4 + (x + i) % 4 for i in range(1, 4)]
    sibling = row_dev((row + 4) % 8)

    local = [
        pltpu.make_async_copy(k, col.at[c, me, 0], lsem.at[0]),
        pltpu.make_async_copy(v, col.at[c, me, 1], lsem.at[1]),
    ]

    def tile(ref, p):
        return ref.at[:, p % 4, :, pl.ds(pl.multiple_of((p // 4) * HD, HD), HD)]

    local += [
        pltpu.make_async_copy(tile(q, me), gch.at[me, 0], lsem.at[2]),
        pltpu.make_async_copy(tile(d, me), gch.at[me, 1], lsem.at[3]),
    ]
    for cp in local:
        cp.start()
    barrier = pltpu.get_barrier_semaphore()

    def hello(i, carry):
        pl.semaphore_signal(barrier, inc=1, device_id=plane_dev((me + i) % PLANE), device_id_type=MESH)
        return carry

    lax.fori_loop(1, PLANE, hello, 0)
    others = [row_dev(r) for r in row_peers] + [shard_dev(nxt), shard_dev(prv)]
    for dev in others:
        pl.semaphore_signal(barrier, inc=1, device_id=dev, device_id_type=MESH)
    pl.semaphore_wait(barrier, PLANE - 1 + len(others))
    for cp in local:
        cp.wait()

    to_next = remote(
        col.at[c, me, :, 1], near.at[0], ssem.at[0], rsem.at[0], shard_dev(nxt)
    )
    to_prev = remote(
        col.at[c, me, :, 0], near.at[1], ssem.at[1], rsem.at[1], shard_dev(prv)
    )
    rand_copy = remote(rand_any, rand_sib, ssem.at[2], rsem.at[2], sibling)

    def pass_on(kv):
        def arrived(py, pz):
            ref = col.at[c, py * NZ + pz, kv]
            remote(ref, ref, ssem.at[3 + kv], rsem.at[3 + kv], sibling).start()

        return arrived

    def piece(kv):
        return lambda py, pz: col.at[c, py * NZ + pz, kv]

    def half(kv):
        return lambda py, pz, h: col.at[c, py * NZ + pz, kv, h]

    flow_k = gather_flow(piece(0), half(0), ("y", "z"), (x, y, z), c, (a_ssem, a_rsem), pass_on(0))
    flow_v = gather_flow(piece(1), half(1), ("z", "y"), (x, y, z), c, (b_ssem, b_rsem), pass_on(1))
    next(flow_k)
    next(flow_v)
    pass_on(0)(y, z)
    pass_on(1)(y, z)

    def send_tiles(i, carry):
        p = (me + i) % PLANE
        remote(tile(q, p), gch.at[me, 0], ssem.at[5], rsem.at[5], plane_dev(p)).start()
        remote(tile(d, p), gch.at[me, 1], ssem.at[5], rsem.at[5], plane_dev(p)).start()
        return carry

    lax.fori_loop(1, PLANE, send_tiles, 0)
    to_next.start()
    to_prev.start()
    rand_copy.start()

    for j in range(2):
        for h in range(HEADS):
            rows = pl.ds(j * 512 + h * 64, 64)
            qs[rows, :] = q[j, :, :, h * HD : (h + 1) * HD].reshape(64, HD)
            ds_[rows, :] = d[j, :, :, h * HD : (h + 1) * HD].reshape(64, HD)

    run_rounds(flow_k, flow_v)
    tiles_in = remote(gch.at[pl.ds(0, 31)], gch.at[pl.ds(0, 31)], ssem.at[5], rsem.at[5], sibling)
    tiles_in.wait_recv()

    g_place = [place(glob[g]) for g in range(2)]
    for g in range(2):
        gx, gc, gpl, gh = g_place[g]
        for t in range(2):
            sel[row, g, t] = gch[gpl, t, gh]
    for r in row_peers:
        remote(sel.at[row], sel.at[row], ssem.at[6], rsem.at[6], row_dev(r)).start()

    for kv in range(2):
        remote(col.at[1 - c, :, kv], col.at[1 - c, :, kv], ssem.at[3 + kv], rsem.at[3 + kv], sibling).wait_recv()

    def wanted(ka_of, slot):
        if slot >= 6:
            return glob[slot - 6]
        return rand[ka_of * 2 + slot // 3, slot % 3]

    for i in range(1, 4):
        xd = (x + i) % 4
        for slot in range(SLOTS):
            bx, bc, bp, bh = place(wanted(zh * 4 + xd, slot))
            for kv in range(2):
                xsend[i - 1, slot, kv] = col[bc, bp, kv, bh]
        remote(xsend.at[i - 1], xbuf.at[x], ssem.at[7], rsem.at[7], row_dev(c * 4 + xd)).start()
    for slot in range(SLOTS):
        bx, bc, bp, bh = place(wanted(ka, slot))
        for kv in range(2):
            xbuf[x, slot, kv] = col[bc, bp, kv, bh]

    remote(sel.at[pl.ds(0, 7)], sel.at[pl.ds(0, 7)], ssem.at[6], rsem.at[6], sibling).wait_recv()
    for g in range(2):
        gx, gc, gpl, gh = g_place[g]
        gq[pl.ds(g * 16, 16), :] = sel[gc * 4 + gx, g, 0]
        gd[pl.ds(g * 16, 16), :] = sel[gc * 4 + gx, g, 1]

    def g_scores(p, carry):
        lanes = pl.ds(pl.multiple_of(p * HD, HD), HD)
        sg[:, lanes] = nt(gq[...], col[c, p, 0].reshape(HD, HD)) * SCALE
        dpg[:, lanes] = nt(gd[...], col[c, p, 1].reshape(HD, HD))
        return carry

    lax.fori_loop(0, PLANE, g_scores, 0)
    g_max = jnp.max(sg[...], axis=1, keepdims=True)
    g_exp = jnp.exp(sg[...] - g_max)
    g_sum = jnp.sum(g_exp, axis=1, keepdims=True)
    g_dot = jnp.sum(g_exp * dpg[...], axis=1, keepdims=True)
    lane = lax.broadcasted_iota(jnp.int32, (32, HD), 1)
    stat[row] = jnp.where(lane == 0, g_max, jnp.where(lane == 1, g_sum, g_dot))
    for r in row_peers:
        remote(stat.at[row], stat.at[row], ssem.at[8], rsem.at[8], row_dev(r)).start()

    to_next.wait_recv()
    to_prev.wait_recv()
    remote(xbuf.at[pl.ds(0, 3)], xbuf.at[pl.ds(0, 3)], ssem.at[7], rsem.at[7], sibling).wait_recv()
    slot_of = lax.broadcasted_iota(jnp.int32, (1, 512), 1) // BLOCK
    lo, hi = pl.ds(0, BLOCK), pl.ds(BLOCK, BLOCK)
    for j in range(2):
        block = shard * 2 + j
        cand = [block - 1, block, block + 1, glob[0], glob[1]]
        cand += [rand[ka * 2 + j, r] for r in range(3)]
        for kv, dst in ((0, kc), (1, vc)):
            near_refs = [near.at[0, kv], col.at[c, me, kv, 0], col.at[c, me, kv, 1], near.at[1, kv]]
            for i in range(3):
                dst[i * BLOCK : (i + 1) * BLOCK, :] = near_refs[i + j][...]
            for i in range(3, 8):
                slot = 6 + i - 3 if i < 5 else j * 3 + i - 5
                dst[i * BLOCK : (i + 1) * BLOCK, :] = xbuf[place(cand[i])[0], slot, kv]
        cands = jnp.zeros((1, 512), jnp.int32)
        for i in range(8):
            cands = jnp.where(slot_of == i, cand[i], cands)
        out = (cands < 0) | (cands >= NBLK)
        for i in range(7):
            out = out | ((slot_of > i) & (cands == cand[i]))
        bias = jnp.where(out, NEG, 0.0)
        blocks = jnp.full((256, 1), block, jnp.int32)
        keep = jnp.where((blocks == glob[0]) | (blocks == glob[1]), 0.0, 1.0)
        for part_i in range(2):
            rows = pl.ds(j * 512 + part_i * 256, 256)
            qv, dv = qs[rows, :], ds_[rows, :]
            s = nt(qv, kc[...]) * SCALE + bias
            e = jnp.exp(s - jnp.max(s, axis=1, keepdims=True))
            w = e * (keep / jnp.sum(e, axis=1, keepdims=True))
            wb = w.astype(BF16)
            o = nn(wb, vc[...]).astype(BF16)
            dot = jnp.sum(dv.astype(F32) * o.astype(F32), axis=1, keepdims=True)
            ds = (w * (nt(dv, vc[...]) - dot)).astype(BF16)
            dqv = (nn(ds, kc[...]) * SCALE).astype(BF16)
            for h in range(4):
                cols = slice((part_i * 4 + h) * HD, (part_i * 4 + h + 1) * HD)
                att[j, :, :, cols] = o[h * 64 : (h + 1) * 64].reshape(4, 16, HD)
                dq[j, :, :, cols] = dqv[h * 64 : (h + 1) * 64].reshape(4, 16, HD)
            dk_new, dv_new = tn(ds, qv) * SCALE, tn(wb, dv)
            if part_i == 0:
                dkv[0], dkv[1] = dk_new, dv_new
            else:
                dkv[0] += dk_new
                dkv[1] += dv_new
        for kv in range(2):
            for i in range(8):
                term = dkv[kv, i * BLOCK : (i + 1) * BLOCK, :]
                spot = i + j - 1
                if i < 3 and spot in (-1, 2):
                    near_send[0 if spot == -1 else 1, kv] = term.astype(BF16)
                elif i < 3:
                    if (j, i) in ((0, 1), (0, 2)):
                        own_sum[kv, pl.ds(spot * BLOCK, BLOCK), :] = term
                    else:
                        own_sum[kv, pl.ds(spot * BLOCK, BLOCK), :] += term
                elif i >= 5:
                    cbuf[row, j * 3 + i - 5, kv] = term.astype(BF16)
                elif j == 0:
                    own_sum[2 + kv, pl.ds((i - 3) * BLOCK, BLOCK), :] = term
                else:
                    total = own_sum[2 + kv, pl.ds((i - 3) * BLOCK, BLOCK), :] + term
                    cbuf[row, 6 + i - 3, kv] = total.astype(BF16)

    def c_copy(src, h, step, sem):
        ref = cbuf.at[src] if h is None else cbuf.at[src, pl.ds(h * 4, 4)]
        dev = sibling if step is None else row_dev(c * 4 + (x + step + 4) % 4)
        return remote(ref, ref, c_ssem.at[sem], c_rsem.at[sem], dev)

    at_x = lambda o: c * 4 + (x + o + 4) % 4
    to_back = remote(near_send.at[0], near_got.at[1], ssem.at[9], rsem.at[9], shard_dev(prv))
    to_fore = remote(near_send.at[1], near_got.at[0], ssem.at[10], rsem.at[10], shard_dev(nxt))
    c_sends = [c_copy(row, None, 1, 0), c_copy(row, None, -1, 1), c_copy(row, None, None, 4)]
    for cp in c_sends:
        cp.start()
    to_back.start()
    to_fore.start()

    remote(stat.at[pl.ds(0, 7)], stat.at[pl.ds(0, 7)], ssem.at[8], rsem.at[8], sibling).wait_recv()
    stats = [stat[i] for i in range(8)]
    top = stats[0][:, 0:1]
    for i in range(1, 8):
        top = jnp.maximum(top, stats[i][:, 0:1])
    total, dot = jnp.zeros((32, 1), F32), jnp.zeros((32, 1), F32)
    for i in range(8):
        f = jnp.exp(stats[i][:, 0:1] - top)
        total += stats[i][:, 1:2] * f
        dot += stats[i][:, 2:3] * f
    g_row = lax.broadcasted_iota(jnp.int32, (32, 1), 0)
    g_one = jnp.full((32, 1), glob[1], jnp.int32)
    first = jnp.where((g_row >= 16) & (g_one == glob[0]), 0.0, 1.0)
    gw = jnp.exp(sg[...] - top) * (first / total)
    gp[...] = gw.astype(BF16)
    gs[...] = (gw * (dpg[...] - dot / total)).astype(BF16)

    def g_out(p, carry):
        lanes = pl.ds(pl.multiple_of(p * HD, HD), HD)
        o, dqv = carry
        return o + nn(gp[:, lanes], col[c, p, 1].reshape(HD, HD)), dqv + nn(gs[:, lanes], col[c, p, 0].reshape(HD, HD))

    zero = jnp.zeros((32, HD), F32)
    g_o, g_dq = lax.fori_loop(0, PLANE, g_out, (zero, zero))
    part[row, 0] = g_o
    part[row, 1] = g_dq * SCALE
    for r in row_peers:
        remote(part.at[row], part.at[row], ssem.at[11], rsem.at[11], row_dev(r)).start()

    c_copy(at_x(-1), None, 1, 0).wait_recv()
    c_copy(at_x(1), None, -1, 1).wait_recv()
    more = [
        c_copy(at_x(-1), 0, 1, 2), c_copy(at_x(1), 1, -1, 3),
        c_copy(at_x(-1), None, None, 5), c_copy(at_x(1), None, None, 6),
    ]
    for cp in more:
        cp.start()
    c_sends += more
    c_copy(at_x(2), 0, 1, 2).wait_recv()
    c_copy(at_x(2), 1, -1, 3).wait_recv()
    last = c_copy(at_x(2), None, None, 7)
    last.start()
    c_sends.append(last)

    remote(part.at[pl.ds(0, 7)], part.at[pl.ds(0, 7)], ssem.at[11], rsem.at[11], sibling).wait_recv()
    for t in range(2):
        acc = part[0, t]
        for i in range(1, 8):
            acc += part[i, t]
        for g in range(2):
            gout[t, g] = acc[g * 16 : (g + 1) * 16].astype(BF16)
    to_back.wait_recv()
    to_fore.wait_recv()
    for kv in range(2):
        near_sum[kv, lo, :] = own_sum[kv, lo, :] + near_got[0, kv].astype(F32)
        near_sum[kv, hi, :] = own_sum[kv, hi, :] + near_got[1, kv].astype(F32)

    def at_other(o):
        return (1 - c) * 4 + (x + o + 4) % 4

    for sem, o in ((4, 0), (5, -1), (6, 1), (7, 2)):
        c_copy(at_other(o), None, None, sem).wait_recv()
    out_copy = pltpu.make_async_copy(cbuf, contrib, lsem.at[0])
    out_copy.start()
    out_copy.wait()
    rand_copy.wait_recv()

    for cp in c_sends + [to_next, to_prev, rand_copy, to_back, to_fore]:
        cp.wait_send()
    for kv in range(2):
        remote(col.at[c, :, kv], col.at[c, :, kv], ssem.at[3 + kv], rsem.at[3 + kv], sibling).wait_send()
    tiles_in.wait_send()
    for ref, sem, n in ((sel, 6, 7), (xbuf, 7, 3), (stat, 8, 7), (part, 11, 7)):
        remote(ref.at[pl.ds(0, n)], ref.at[pl.ds(0, n)], ssem.at[sem], rsem.at[sem], sibling).wait_send()


def kernel_b(rand, rand_sib, glob, contrib, gp, gs, gq, gd, out, acc):
    x, y, z, c = here()
    zh = z // 4

    def dense(p, carry):
        lanes = pl.ds(pl.multiple_of(p * HD, HD), HD)
        acc[p, 0] = tn(gs[:, lanes], gq[...]) * SCALE
        acc[p, 1] = tn(gp[:, lanes], gd[...])
        return carry

    lax.fori_loop(0, PLANE, dense, 0)
    for core in range(2):
        for xs in range(NX):
            for slot in range(SLOTS):
                if slot >= 6:
                    block = glob[slot - 6]
                else:
                    r, s = (zh * 4 + xs) * 2 + slot // 3, slot % 3
                    block = jnp.where(c == core, rand[r, s], rand_sib[r, s])
                bx, bc, bp, bh = place(block)

                @pl.when((bx == x) & (bc == c))
                def _(core=core, xs=xs, slot=slot, bp=bp, bh=bh):
                    rows = pl.ds(pl.multiple_of(bh * BLOCK, BLOCK), BLOCK)
                    src = jnp.where(core == 0, 0, 4) + xs
                    acc[bp, :, rows, :] += contrib[src, slot].astype(F32)

    def narrow(p, carry):
        out[p] = acc[p].astype(BF16)
        return carry

    lax.fori_loop(0, PLANE, narrow, 0)


def kernel_c(
    glob, acc, near_sum, att_in, dq_in, gout,
    att, dq, dk, dv,
    got_k, out_k, got_v, out_v, gall,
    k_ssem, k_rsem, v_ssem, v_rsem, o_ssem, o_rsem, w_ssem, w_rsem, lsem,
):
    x, y, z, c = here()
    me = y * NZ + z
    shard = lax.axis_index("pb") * 8 + lax.axis_index("ka")
    own = pltpu.make_async_copy(gout, gall.at[me], lsem.at[0])
    own.start()
    greet(
        [
            device(x, (y + 1) % NY, z, c), device(x, (y + NY - 1) % NY, z, c),
            device(x, y, (z + 1) % NZ, c), device(x, y, (z + NZ - 1) % NZ, c),
        ]
    )
    own.wait()
    pos = (x, y, z)

    def finish(kv, dst):
        def done(value):
            dst[...] = (value + near_sum[kv]).astype(BF16)

        return done

    def term(kv):
        return lambda py, pz: acc.at[py * NZ + pz, kv]

    def piece(t):
        return lambda py, pz: gall.at[py * NZ + pz, t]

    def half(t):
        return lambda py, pz, h: gall.at[py * NZ + pz, t, h]

    nothing = lambda py, pz: None
    run_rounds(
        reduce_flow(term(0), got_k, out_k, ("z", "y"), pos, c, (k_ssem, k_rsem), finish(0, dk)),
        reduce_flow(term(1), got_v, out_v, ("y", "z"), pos, c, (v_ssem, v_rsem), finish(1, dv)),
        gather_flow(piece(0), half(0), ("y", "z"), pos, c, (o_ssem, o_rsem), nothing),
        gather_flow(piece(1), half(1), ("z", "y"), pos, c, (w_ssem, w_rsem), nothing),
    )
    for j in range(2):
        blocks = jnp.full((16, HD), shard * 2 + j, jnp.int32)
        is_glob = [blocks == glob[g] for g in range(2)]
        for t, src, dst in ((0, att_in, att), (1, dq_in, dq)):
            for p in range(PLANE):
                cols = slice((p // 4) * HD, (p // 4 + 1) * HD)
                value = jnp.where(is_glob[1], gall[p, t, 1], src[j, p % 4, :, cols])
                dst[j, p % 4, :, cols] = jnp.where(is_glob[0], gall[p, t, 0], value)


def body(queries, key_vectors, value_vectors, out_grad, rand_blocks, global_blocks):
    vmem = pl.BlockSpec(memory_space=pltpu.VMEM)
    smem = pl.BlockSpec(memory_space=pltpu.SMEM)
    hbm = pl.BlockSpec(memory_space=pl.ANY)
    shape = jax.ShapeDtypeStruct
    dma = pltpu.SemaphoreType.DMA
    q4 = queries.reshape(2, 4, 16, HEADS * HD)
    d4 = out_grad.reshape(2, 4, 16, HEADS * HD)
    yz, zy = ("y", "z"), ("z", "y")
    ga, gb = GATHER_SEMS[yz], GATHER_SEMS[zy]
    att, dq, contrib, gp, gs, gq, gd, near_sum, gout, rand_sib = pl.pallas_call(
        kernel_a,
        name="exchange_and_attend",
        out_shape=(
            shape((2, 4, 16, HEADS * HD), BF16),
            shape((2, 4, 16, HEADS * HD), BF16),
            shape((8, SLOTS, 2, BLOCK, HD), BF16),
            shape((32, PLANE * HD), BF16),
            shape((32, PLANE * HD), BF16),
            shape((32, HD), BF16),
            shape((32, HD), BF16),
            shape((2, HD, HD), F32),
            shape((2, 2, 16, HD), BF16),
            shape((16, 3), jnp.int32),
        ),
        in_specs=[smem, smem, hbm, vmem, vmem, vmem, vmem],
        out_specs=(vmem, vmem, hbm, vmem, vmem, vmem, vmem, vmem, vmem, hbm),
        scratch_shapes=[
            pltpu.VMEM((2, PLANE, 2, 2, BLOCK, HD), BF16),
            pltpu.VMEM((PLANE, 2, 2, 16, HD), BF16),
            pltpu.VMEM((8, 2, 2, 16, HD), BF16),
            pltpu.VMEM((4, SLOTS, 2, BLOCK, HD), BF16),
            pltpu.VMEM((3, SLOTS, 2, BLOCK, HD), BF16),
            pltpu.VMEM((2, 2, BLOCK, HD), BF16),
            pltpu.VMEM((2, 2, BLOCK, HD), BF16),
            pltpu.VMEM((2, 2, BLOCK, HD), BF16),
            pltpu.VMEM((8, SLOTS, 2, BLOCK, HD), BF16),
            pltpu.VMEM((8, 32, HD), F32),
            pltpu.VMEM((8, 2, 32, HD), F32),
            pltpu.VMEM((32, PLANE * HD), F32),
            pltpu.VMEM((32, PLANE * HD), F32),
            pltpu.VMEM((512, HD), BF16),
            pltpu.VMEM((512, HD), BF16),
            pltpu.VMEM((1024, HD), BF16),
            pltpu.VMEM((1024, HD), BF16),
            pltpu.VMEM((2, 512, HD), F32),
            pltpu.VMEM((4, HD, HD), F32),
            dma((ga,)), dma((ga,)), dma((gb,)), dma((gb,)), dma((8,)), dma((8,)),
            dma((12,)), dma((12,)), dma((4,)),
        ],
        compiler_params=pltpu.CompilerParams(collective_id=0, has_side_effects=True),
    )(
        rand_blocks, global_blocks, rand_blocks, q4,
        key_vectors.reshape(2, BLOCK, HD), value_vectors.reshape(2, BLOCK, HD), d4,
    )
    acc = pl.pallas_call(
        kernel_b,
        name="spread_terms",
        out_shape=shape((PLANE, 2, HD, HD), BF16),
        in_specs=[smem, smem, smem, vmem, vmem, vmem, vmem, vmem],
        out_specs=vmem,
        scratch_shapes=[pltpu.VMEM((PLANE, 2, HD, HD), F32)],
    )(rand_blocks, rand_sib, global_blocks, contrib, gp, gs, gq, gd)
    mk, mv = REDUCE_MSGS[zy], REDUCE_MSGS[yz]
    att, dq, dk, dv = pl.pallas_call(
        kernel_c,
        name="reduce_and_finish",
        out_shape=(
            shape((2, 4, 16, HEADS * HD), BF16),
            shape((2, 4, 16, HEADS * HD), BF16),
            shape((HD, HD), BF16),
            shape((HD, HD), BF16),
        ),
        in_specs=[smem] + [vmem] * 5,
        out_specs=(vmem,) * 4,
        scratch_shapes=[
            pltpu.VMEM((mk, HD, HD), BF16), pltpu.VMEM((mk, HD, HD), BF16),
            pltpu.VMEM((mv, HD, HD), BF16), pltpu.VMEM((mv, HD, HD), BF16),
            pltpu.VMEM((PLANE, 2, 2, 16, HD), BF16),
            dma((mk,)), dma((mk,)), dma((mv,)), dma((mv,)),
            dma((ga,)), dma((ga,)), dma((gb,)), dma((gb,)), dma((1,)),
        ],
        compiler_params=pltpu.CompilerParams(collective_id=1, has_side_effects=True),
    )(global_blocks, acc, near_sum, att, dq, gout)
    return att.reshape(queries.shape), dq.reshape(queries.shape), dk, dv


def solution(mesh):
    assert (mesh.shape["pb"], mesh.shape["ka"]) == (32, 8)
    rows = P(("pb", "ka"), None)
    return jax.shard_map(
        body,
        mesh=mesh,
        in_specs=(rows, rows, rows, rows, P("pb", None), P()),
        out_specs=(rows, rows, rows, rows),
        check_vma=False,
    )
```

```python
import math

import jax
import jax.numpy as jnp
from jax import lax
from jax.experimental import pallas as pl
from jax.experimental.pallas import tpu as pltpu
from jax.sharding import PartitionSpec as P

NX, NY, NZ = 4, 4, 8
PLANE = NY * NZ
SHARDS = 256
NBLK = 512
BLOCK = 64
HD = 128
HEADS = 8
SLOTS = 8
SCALE = 1.0 / math.sqrt(HD)
NEG = -1e30
VMEM_A, VMEM_B, VMEM_C, VMEM_D = 28 << 20, 14 << 20, 14 << 20, 8 << 20
MESH = pl.DeviceIdType.MESH
F32, BF16 = jnp.float32, jnp.bfloat16


def here():
    pb, ka = lax.axis_index("pb"), lax.axis_index("ka")
    return ka % 4, pb // 8, (ka // 4) * 4 + (pb // 2) % 4, pb % 2


def device(x, y, z, c):
    return ((y * 4 + z % 4) * 2 + c, (z // 4) * 4 + x)


def place(block):
    shard = block // 2
    pb, ka = shard // 8, shard % 8
    return ka % 4, pb % 2, (pb // 8) * 8 + (ka // 4) * 4 + (pb // 2) % 4, block % 2


def remote(src, dst, ssem, rsem, dev):
    return pltpu.make_async_remote_copy(
        src_ref=src, dst_ref=dst, send_sem=ssem, recv_sem=rsem, device_id=dev, device_id_type=MESH
    )


RATE, LATENCY, AHEAD = 37.0, 1.6, 2.0


def schedule(msgs):
    depth = [1] * len(msgs)
    for i in range(len(msgs) - 1, -1, -1):
        for dep in msgs[i][0]:
            depth[dep] = max(depth[dep], depth[i] + 1)
    ranked = sorted(range(len(msgs)), key=lambda i: (-depth[i], i))
    now, free, arrival, come, order = 0.0, {}, {}, set(), []
    while len(come) < len(msgs):
        for i in ranked:
            deps, link, size, work = msgs[i][:4]
            begin = max(free.get(link, 0.0), now)
            if i in arrival or begin > now + AHEAD or any(dep not in come for dep in deps):
                continue
            now += work
            free[link] = max(begin, now) + size / RATE
            arrival[i] = free[link] + LATENCY
            order.append(("send", i))
        i = min((i for i in arrival if i not in come), key=lambda i: (arrival[i], i))
        now = max(now, arrival[i]) + 0.05
        come.add(i)
        order.append(("wait", i))
    return order


def play(*flows):
    msgs = []
    for own, end in flows:
        base = len(msgs)
        msgs += [([dep + base for dep in m[0]],) + m[1:] for m in own]
    for what, i in schedule(msgs):
        msgs[i][4 if what == "send" else 5]()
    for own, end in flows:
        end()


def ring_around(order, pos, core):
    x, y, z = pos

    def at(o1, o2):
        oy, oz = (o1, o2) if order[0] == "y" else (o2, o1)
        return (y + oy + NY) % NY, (z + oz + NZ) % NZ

    def dev(axis, d):
        step = 1 if d == 0 else -1
        if axis == "y":
            return device(x, (y + step + NY) % NY, z, core)
        return device(x, y, (z + step + NZ) % NZ, core)

    return at, dev, RING[order[0]], RING[order[1]]


RING = {"y": NY, "z": NZ}


def gather_flow(piece, half, order, pos, core, sems, arrived, kb, whole):
    ssem, rsem = sems
    at, dev, n1, n2 = ring_around(order, pos, core)
    msgs, index, seen = [], {}, {}

    def message(deps, o1, o2, nxt, d, halved, axis):
        i = len(msgs)

        def copy(a, b):
            cy, cz = at(a, b)
            ref = half(cy, cz, d) if halved else piece(cy, cz)
            return remote(ref, ref, ssem.at[0], rsem.at[i], dev(axis, d))

        def send():
            copy(o1, o2).start()

        def wait():
            copy(*nxt).wait_recv()
            spot = tuple(abs(o) if abs(o) == n // 2 else o for o, n in zip(nxt, (n1, n2)))
            seen[spot] = seen.get(spot, 0) + 1
            if seen[spot] == (2 if halved else 1):
                arrived(*at(*nxt))

        msgs.append((deps, (axis, d), kb / 2 if halved else kb, 0.02, send, wait))
        return i

    for k in range(n1 // 2):
        for d in (0, 1):
            sign = -1 if d == 0 else 1
            deps = [index[1, sign * k, d]] if k else []
            i = message(deps, sign * k, 0, (sign * (k + 1), 0), d, k == n1 // 2 - 1, order[0])
            index[1, sign * (k + 1), d] = i
    offsets = [0] + [s * k for k in range(1, n1 // 2) for s in (-1, 1)] + [n1 // 2]
    for o in offsets:
        if o == 0:
            first = []
        elif o == n1 // 2:
            first = [index[1, -o, 0], index[1, o, 1]]
        else:
            first = [index[1, o, 0 if o < 0 else 1]]
        for k in range(n2 // 2):
            for d in (0, 1):
                sign = -1 if d == 0 else 1
                deps = [index[2, o, sign * k, d]] if k else first
                i = message(deps, o, sign * k, (o, sign * (k + 1)), d, k == n2 // 2 - 1, order[1])
                index[2, o, sign * (k + 1), d] = i

    def end():
        remote(whole, whole, ssem.at[0], rsem.at[0], dev("y", 0)).wait_send()

    return msgs, end


GATHER_SEMS = {("y", "z"): NY + NY * NZ, ("z", "y"): NZ + NZ * NY}


def reduce_flow(own, got, out, order, pos, core, sems, done, kb):
    ssem, rsem = sems
    at, dev, n1, n2 = ring_around(order, pos, core)
    rows = got.shape[1] // 2
    msgs = []

    def half_of(ref, d):
        return ref.at[pl.ds(d * rows, rows)]

    def load(ref, h):
        return (ref[...] if h is None else half_of(ref, h)[...]).astype(F32)

    def ring(n, axis, term, deps_of):
        steps = n // 2
        base = len(msgs)
        for d in (0, 1):
            for t in range(steps):
                o = (1 if d == 0 else -1) * (steps - t)
                i = base + d * steps + t
                deps = list(deps_of(o)) + ([i - 1] if t else [])

                def copy(i=i, t=t, d=d):
                    src, dst = out.at[i], got.at[i]
                    if t == 0:
                        src, dst = half_of(src, d), half_of(dst, d)
                    return remote(src, dst, ssem.at[0], rsem.at[i], dev(axis, d))

                def send(i=i, o=o, t=t, d=d, copy=copy):
                    value = term(o)
                    if t == 0:
                        half_of(out.at[i], d)[...] = value(d).astype(BF16)
                    elif t == 1:
                        half_of(out.at[i], d)[...] = (value(d) + load(got.at[i - 1], d)).astype(BF16)
                        half_of(out.at[i], 1 - d)[...] = value(1 - d).astype(BF16)
                    else:
                        out[i] = (value(None) + load(got.at[i - 1], None)).astype(BF16)
                    copy().start()

                def wait(copy=copy):
                    copy().wait_recv()

                msgs.append((deps, (axis, d), kb if t else kb / 2, 0.005 * kb, send, wait))
        return base

    offsets = [n2 // 2] + [s * k for k in range(n2 // 2 - 1, 0, -1) for s in (-1, 1)] + [0]
    ends = {}
    for o2 in offsets:

        def term(o1, o2=o2):
            ref = own(*at(o1, o2))
            return lambda h: load(ref, h)

        base = ring(n1, order[0], term, lambda o: [])
        ends[o2] = (base + n1 // 2 - 1, base + n1 - 1)
    ends[-(n2 // 2)] = ends[n2 // 2]

    def term2(o2):
        a, b = ends[o2]
        ref = own(*at(0, o2))
        return lambda h: load(ref, h) + load(got.at[a], h) + load(got.at[b], h)

    base = ring(n2, order[1], term2, lambda o: ends[o])

    def end():
        last = (base + n2 // 2 - 1, base + n2 - 1)
        done(term2(0)(None) + load(got.at[last[0]], None) + load(got.at[last[1]], None))
        whole = out.at[pl.ds(0, PLANE - 1)]
        remote(whole, whole, ssem.at[0], rsem.at[0], dev("y", 0)).wait_send()

    return msgs, end


REDUCE_MSGS = {("y", "z"): NY * NZ + NZ, ("z", "y"): NZ * NY + NY}


def greet(devices):
    barrier = pltpu.get_barrier_semaphore()
    for dev in devices:
        pl.semaphore_signal(barrier, inc=1, device_id=dev, device_id_type=MESH)
    pl.semaphore_wait(barrier, len(devices))


def nt(a, b):
    return lax.dot_general(a, b, (((1,), (1,)), ((), ())), preferred_element_type=F32)


def tn(a, b):
    return lax.dot_general(a, b, (((0,), (0,)), ((), ())), preferred_element_type=F32)


def nn(a, b):
    return lax.dot_general(a, b, (((1,), (0,)), ((), ())), preferred_element_type=F32)


def kernel_a(
    rand_any, glob_any, q_any, k, v, d_any,
    att, dq, contrib, dense, near_sum, gout, rand_sib,
    col, gown, g_got, g_out_buf, sel, xm, xs, xall, stat, part,
    rand, glob, q, d, sg, dpg, gp, gs, gq, gd, kc, vc, qs, ds_, dkv, own_sum,
    a_ssem, a_rsem, b_ssem, b_rsem, g_ssem, g_rsem, c_ssem, c_rsem, x_ssem, x_rsem, ssem, rsem, lsem,
):
    x, y, z, c = here()
    pb, ka = lax.axis_index("pb"), lax.axis_index("ka")
    shard = pb * 8 + ka
    me = y * NZ + z
    row = c * 4 + x
    zh = z // 4
    pos = (x, y, z)

    def row_dev(r):
        return device(r % 4, y, z, r // 4)

    def x_dev(step):
        return device((x + step + 4) % 4, y, z, c)

    row_peers = [(row + i) % 8 for i in range(1, 8)]
    sibling = row_dev((row + 4) % 8)

    local = [
        pltpu.make_async_copy(k, col.at[c, me, 0], lsem.at[0]),
        pltpu.make_async_copy(v, col.at[c, me, 1], lsem.at[1]),
        pltpu.make_async_copy(q_any, q, lsem.at[2]),
        pltpu.make_async_copy(d_any, d, lsem.at[3]),
        pltpu.make_async_copy(rand_any, rand, lsem.at[4]),
        pltpu.make_async_copy(glob_any, glob, lsem.at[5]),
    ]
    for cp in local:
        cp.start()
    greet(
        [
            device(x, (y + 1) % NY, z, c), device(x, (y + NY - 1) % NY, z, c),
            device(x, y, (z + 1) % NZ, c), device(x, y, (z + NZ - 1) % NZ, c),
        ]
        + [row_dev(r) for r in row_peers]
    )
    for cp in local:
        cp.wait()
    rand_copy = remote(rand_any, rand_sib, ssem.at[2], rsem.at[2], sibling)
    rand_copy.start()

    def pass_on(kv):
        def arrived(py, pz):
            ref = col.at[c, py * NZ + pz, kv]
            remote(ref, ref, ssem.at[3 + kv], rsem.at[3 + kv], sibling).start()

        return arrived

    def piece(kv):
        return lambda py, pz: col.at[c, py * NZ + pz, kv]

    def half(kv):
        return lambda py, pz, h: col.at[c, py * NZ + pz, kv, h]

    def some(kv):
        return col.at[0, pl.ds(0, PLANE - 1), kv]

    flow_k = gather_flow(
        piece(0), half(0), ("y", "z"), pos, c, (a_ssem, a_rsem), pass_on(0), 32, some(0)
    )
    flow_v = gather_flow(
        piece(1), half(1), ("z", "y"), pos, c, (b_ssem, b_rsem), pass_on(1), 32, some(1)
    )
    pass_on(0)(y, z)
    pass_on(1)(y, z)

    g_place = [place(glob[g]) for g in range(2)]
    shards = jnp.full((16, HD), shard, jnp.int32)
    for g in range(2):
        mine = shards == glob[g] // 2
        for t, ref in ((0, q), (1, d)):
            for p in range(PLANE):
                value = ref[g_place[g][3], p % 4, :, (p // 4) * HD : (p // 4 + 1) * HD]
                rows = slice((g * 2 + t) * 16, (g * 2 + t + 1) * 16)
                gown[p, rows, :] = jnp.where(mine, value, jnp.zeros_like(value))

    def tiles_done(value):
        sel[row] = value.reshape(2, 2, 16, HD).astype(BF16)

    flow_g = reduce_flow(
        lambda py, pz: gown.at[py * NZ + pz], g_got, g_out_buf, ("y", "z"), pos, c, (g_ssem, g_rsem),
        tiles_done, 16,
    )

    for j in range(2):
        for h in range(HEADS):
            rows = pl.ds(j * 512 + h * 64, 64)
            qs[rows, :] = q[j, :, :, h * HD : (h + 1) * HD].reshape(64, HD)
            ds_[rows, :] = d[j, :, :, h * HD : (h + 1) * HD].reshape(64, HD)

    play(flow_k, flow_v, flow_g)
    for r in row_peers:
        remote(sel.at[row], sel.at[row], ssem.at[6], rsem.at[6], row_dev(r)).start()

    for kv in range(2):
        remote(col.at[1 - c, :, kv], col.at[1 - c, :, kv], ssem.at[3 + kv], rsem.at[3 + kv], sibling).wait_recv()

    def wanted(ka_of, slot):
        if slot >= 6:
            return glob[slot - 6]
        return rand[slot % 3, ka_of * 2 + slot // 3]

    def ka_at(step):
        return zh * 4 + (x + step + 4) % 4

    def slot_at(direction, i):
        return i if direction == 0 else (i + 4) % 8

    for dr in range(2):
        for i in range(4):
            bx, bc, bp, bh = place(wanted(ka_at(2), slot_at(dr, i)))
            for kv in range(2):
                xs[dr, 9 + i, kv] = col[bc, bp, kv, bh]
    for dr in range(2):
        remote(
            xs.at[dr, pl.ds(9, 4)], xm.at[dr, 0], x_ssem.at[dr], x_rsem.at[dr], x_dev(1 - 2 * dr)
        ).start()
    for dr in range(2):
        step = 1 - 2 * dr
        for i in range(8):
            bx, bc, bp, bh = place(wanted(ka_at(step), slot_at(dr, i)))
            for kv in range(2):
                if i < 4:
                    xm[dr, 1, i, kv] = col[bc, bp, kv, bh]
                else:
                    xs[dr, i, kv] = col[bc, bp, kv, bh]
        to = pb * 8 + ka_at(step)
        edge = (to * 2 + 2 * SHARDS - 1) % NBLK if dr == 0 else (to * 2 + 2) % NBLK
        bx, bc, bp, bh = place(edge)
        for kv in range(2):
            xs[dr, 8, kv] = col[bc, bp, kv, bh]
        remote(
            xs.at[dr, pl.ds(4, 5)], xall.at[dr, pl.ds(4, 5)], x_ssem.at[2 + dr], x_rsem.at[2 + dr], x_dev(step)
        ).start()
    for slot in range(SLOTS):
        bx, bc, bp, bh = place(wanted(ka, slot))
        for kv in range(2):
            xall[2, slot, kv] = col[bc, bp, kv, bh]
    for dr in range(2):
        got = xm.at[dr, 0]
        remote(got, got, x_ssem.at[dr], x_rsem.at[dr], x_dev(1)).wait_recv()
    for dr in range(2):
        step = 1 - 2 * dr
        for i in range(4):
            bx = place(wanted(ka_at(step), slot_at(dr, i)))[0]
            which = jnp.where(bx == x, 1, 0)
            for kv in range(2):
                xs[dr, i, kv] = xm[dr, which, i, kv]
        remote(
            xs.at[dr, pl.ds(0, 4)], xall.at[dr, pl.ds(0, 4)], x_ssem.at[4 + dr], x_rsem.at[4 + dr], x_dev(step)
        ).start()

    remote(sel.at[pl.ds(0, 7)], sel.at[pl.ds(0, 7)], ssem.at[6], rsem.at[6], sibling).wait_recv()
    for g in range(2):
        gx, gc, gpl, gh = g_place[g]
        gq[pl.ds(g * 16, 16), :] = sel[gc * 4 + gx, g, 0]
        gd[pl.ds(g * 16, 16), :] = sel[gc * 4 + gx, g, 1]
    for i in range(4):
        lanes, ps = slice(i * 1024, (i + 1) * 1024), pl.ds(i * 8, 8)
        sg[:, lanes] = nt(gq[...], col[c, ps, 0].reshape(1024, HD)) * SCALE
        dpg[:, lanes] = nt(gd[...], col[c, ps, 1].reshape(1024, HD))
    g_max = jnp.max(sg[...], axis=1, keepdims=True)
    g_exp = jnp.exp(sg[...] - g_max)
    g_sum = jnp.sum(g_exp, axis=1, keepdims=True)
    g_dot = jnp.sum(g_exp * dpg[...], axis=1, keepdims=True)
    lane = lax.broadcasted_iota(jnp.int32, (32, HD), 1)
    stat[row] = jnp.where(lane == 0, g_max, jnp.where(lane == 1, g_sum, g_dot))
    for r in row_peers:
        remote(stat.at[row], stat.at[row], ssem.at[8], rsem.at[8], row_dev(r)).start()

    for dr in range(2):
        for lo, n, sem in ((4, 5, 2), (0, 4, 4)):
            ref = xall.at[dr, pl.ds(lo, n)]
            remote(ref, ref, x_ssem.at[sem + dr], x_rsem.at[sem + dr], x_dev(1)).wait_recv()
    slot_of = lax.broadcasted_iota(jnp.int32, (1, 512), 1) // BLOCK
    lo, hi = pl.ds(0, BLOCK), pl.ds(BLOCK, BLOCK)
    for j in range(2):
        block = shard * 2 + j
        cand = [block - 1, block, block + 1, glob[0], glob[1]]
        cand += [rand[r, ka * 2 + j] for r in range(3)]
        for kv, dst in ((0, kc), (1, vc)):
            near_refs = [xall.at[0, 8, kv], col.at[c, me, kv, 0], col.at[c, me, kv, 1], xall.at[1, 8, kv]]
            for i in range(3):
                dst[i * BLOCK : (i + 1) * BLOCK, :] = near_refs[i + j][...]
            for i in range(3, 8):
                slot = 6 + i - 3 if i < 5 else j * 3 + i - 5
                far = 0 if slot < 4 else 1
                off = (place(cand[i])[0] + 4 - x) % 4
                src = jnp.where(off == 0, 2, jnp.where(off == 3, 0, jnp.where(off == 1, 1, far)))
                spot = jnp.where(src == 1, (slot + 4) % 8, slot)
                dst[i * BLOCK : (i + 1) * BLOCK, :] = xall[src, spot, kv]
        cands = jnp.zeros((1, 512), jnp.int32)
        for i in range(8):
            cands = jnp.where(slot_of == i, cand[i], cands)
        out = (cands < 0) | (cands >= NBLK)
        for i in range(7):
            out = out | ((slot_of > i) & (cands == cand[i]))
        bias = jnp.where(out, NEG, 0.0)
        blocks = jnp.full((256, 1), block, jnp.int32)
        keep = jnp.where((blocks == glob[0]) | (blocks == glob[1]), 0.0, 1.0)
        for part_i in range(2):
            rows = pl.ds(j * 512 + part_i * 256, 256)
            qv, dv = qs[rows, :], ds_[rows, :]
            s = nt(qv, kc[...]) * SCALE + bias
            e = jnp.exp(s - jnp.max(s, axis=1, keepdims=True))
            w = e * (keep / jnp.sum(e, axis=1, keepdims=True))
            wb = w.astype(BF16)
            o = nn(wb, vc[...]).astype(BF16)
            dot = jnp.sum(dv.astype(F32) * o.astype(F32), axis=1, keepdims=True)
            ds = (w * (nt(dv, vc[...]) - dot)).astype(BF16)
            dqv = (nn(ds, kc[...]) * SCALE).astype(BF16)
            for h in range(4):
                cols = slice((part_i * 4 + h) * HD, (part_i * 4 + h + 1) * HD)
                att[j, :, :, cols] = o[h * 64 : (h + 1) * 64].reshape(4, 16, HD)
                dq[j, :, :, cols] = dqv[h * 64 : (h + 1) * 64].reshape(4, 16, HD)
            dk_new, dv_new = tn(ds, qv) * SCALE, tn(wb, dv)
            if part_i == 0:
                dkv[0], dkv[1] = dk_new, dv_new
            else:
                dkv[0] += dk_new
                dkv[1] += dv_new
        for kv in range(2):
            for i in range(8):
                term = dkv[kv, i * BLOCK : (i + 1) * BLOCK, :]
                spot = i + j - 1
                if i < 3 and spot in (-1, 2):
                    contrib[row, 9 if spot == -1 else 0, kv] = term.astype(BF16)
                elif i < 3:
                    if (j, i) in ((0, 1), (0, 2)):
                        own_sum[kv, pl.ds(spot * BLOCK, BLOCK), :] = term
                    else:
                        total = own_sum[kv, pl.ds(spot * BLOCK, BLOCK), :] + term
                        near_sum[kv, pl.ds(spot * BLOCK, BLOCK), :] = total
                elif i >= 5:
                    contrib[row, 1 + j * 3 + i - 5, kv] = term.astype(BF16)
                elif j == 0:
                    own_sum[2 + kv, pl.ds((i - 3) * BLOCK, BLOCK), :] = term
                else:
                    total = own_sum[2 + kv, pl.ds((i - 3) * BLOCK, BLOCK), :] + term
                    contrib[row, 7 + i - 3, kv] = total.astype(BF16)

    def c_copy(src, first, n, step, sem):
        ref = contrib.at[src, pl.ds(first, n)]
        dev = sibling if step is None else x_dev(step)
        return remote(ref, ref, c_ssem.at[sem], c_rsem.at[sem], dev)

    def at_x(o):
        return c * 4 + (x + o + 4) % 4

    c_sends = [c_copy(row, 0, 9, 1, 0), c_copy(row, 1, 9, -1, 1), c_copy(row, 1, 8, None, 4)]
    for cp in c_sends:
        cp.start()

    remote(stat.at[pl.ds(0, 7)], stat.at[pl.ds(0, 7)], ssem.at[8], rsem.at[8], sibling).wait_recv()
    stats = [stat[i] for i in range(8)]
    top = stats[0][:, 0:1]
    for i in range(1, 8):
        top = jnp.maximum(top, stats[i][:, 0:1])
    total, dot = jnp.zeros((32, 1), F32), jnp.zeros((32, 1), F32)
    for i in range(8):
        f = jnp.exp(stats[i][:, 0:1] - top)
        total += stats[i][:, 1:2] * f
        dot += stats[i][:, 2:3] * f
    g_row = lax.broadcasted_iota(jnp.int32, (32, 1), 0)
    g_one = jnp.full((32, 1), glob[1], jnp.int32)
    first = jnp.where((g_row >= 16) & (g_one == glob[0]), 0.0, 1.0)
    gw = jnp.exp(sg[...] - top) * (first / total)
    gp[...] = gw.astype(BF16)
    gs[...] = (gw * (dpg[...] - dot / total)).astype(BF16)
    g_o, g_dq = jnp.zeros((32, HD), F32), jnp.zeros((32, HD), F32)
    for i in range(4):
        lanes, ps = slice(i * 1024, (i + 1) * 1024), pl.ds(i * 8, 8)
        g_o += nn(gp[:, lanes], col[c, ps, 1].reshape(1024, HD))
        g_dq += nn(gs[:, lanes], col[c, ps, 0].reshape(1024, HD))
    part[row, 0] = g_o
    part[row, 1] = g_dq * SCALE
    for r in row_peers:
        remote(part.at[row], part.at[row], ssem.at[11], rsem.at[11], row_dev(r)).start()

    c_copy(at_x(-1), 0, 9, 1, 0).wait_recv()
    more = [c_copy(at_x(-1), 1, 4, 1, 2), c_copy(at_x(-1), 0, 9, None, 5)]
    for cp in more:
        cp.start()
    c_copy(at_x(1), 1, 9, -1, 1).wait_recv()
    more += [c_copy(at_x(1), 5, 4, -1, 3), c_copy(at_x(1), 1, 9, None, 6)]
    for cp in more[2:]:
        cp.start()
    c_sends += more

    for i in range(4):
        lanes, ps = slice(i * 1024, (i + 1) * 1024), pl.ds(i * 8, 8)
        dense[ps, 0] = (tn(gs[:, lanes], gq[...]) * SCALE).reshape(8, HD, HD)
        dense[ps, 1] = tn(gp[:, lanes], gd[...]).reshape(8, HD, HD)

    c_copy(at_x(2), 1, 4, 1, 2).wait_recv()
    c_copy(at_x(2), 5, 4, -1, 3).wait_recv()
    last = c_copy(at_x(2), 1, 8, None, 7)
    last.start()
    c_sends.append(last)

    remote(part.at[pl.ds(0, 7)], part.at[pl.ds(0, 7)], ssem.at[11], rsem.at[11], sibling).wait_recv()
    for t in range(2):
        acc = part[0, t]
        for i in range(1, 8):
            acc += part[i, t]
        for g in range(2):
            gout[t, g] = acc[g * 16 : (g + 1) * 16].astype(BF16)

    def at_other(o):
        return (1 - c) * 4 + (x + o + 4) % 4

    for sem, o, first, n in ((4, 0, 1, 8), (5, -1, 0, 9), (6, 1, 1, 9), (7, 2, 1, 8)):
        c_copy(at_other(o), first, n, None, sem).wait_recv()
    rand_copy.wait_recv()

    for cp in c_sends + [rand_copy]:
        cp.wait_send()
    for kv in range(2):
        remote(col.at[c, :, kv], col.at[c, :, kv], ssem.at[3 + kv], rsem.at[3 + kv], sibling).wait_send()
    for ref, sem in ((sel, 6), (stat, 8), (part, 11)):
        remote(ref.at[pl.ds(0, 7)], ref.at[pl.ds(0, 7)], ssem.at[sem], rsem.at[sem], sibling).wait_send()
    for dr in range(2):
        for first, n, sem in ((9, 4, 0), (4, 5, 2), (0, 4, 4)):
            ref = xs.at[dr, pl.ds(first, n)]
            remote(ref, ref, x_ssem.at[sem + dr], x_rsem.at[sem + dr], x_dev(1)).wait_send()


def kernel_b(rand, rand_sib, glob, contrib, dense, acc):
    x, y, z, c = here()
    zh = z // 4
    del dense

    def add(block, here_too, src, entry):
        bx, bc, bp, bh = place(block)

        @pl.when(here_too & (bx == x) & (bc == c))
        def _():
            rows = pl.ds(pl.multiple_of(bh * BLOCK, BLOCK), BLOCK)
            acc[bp, :, rows, :] += contrib[src, entry].astype(F32)

    for core in range(2):
        for xs in range(NX):
            src = core * 4 + xs
            shard = ((y * 4 + z % 4) * 2 + core) * 8 + zh * 4 + xs
            for slot in range(SLOTS):
                if slot >= 6:
                    block = glob[slot - 6]
                else:
                    r, s = (zh * 4 + xs) * 2 + slot // 3, slot % 3
                    block = jnp.where(c == core, rand[s, r], rand_sib[s, r])
                add(block, True, src, 1 + slot)
            after, before = shard * 2 + 2, shard * 2 - 1
            add(jnp.minimum(after, NBLK - 1), (after < NBLK) & ((xs - x + 4) % 4 == 3), src, 0)
            add(jnp.maximum(before, 0), (before >= 0) & ((xs - x + 4) % 4 == 1), src, 9)


def kernel_c(
    acc, gout,
    sums, gall,
    got_k, out_k, got_v, out_v,
    k_ssem, k_rsem, v_ssem, v_rsem, o_ssem, o_rsem, w_ssem, w_rsem, lsem,
):
    x, y, z, c = here()
    me = y * NZ + z
    own = pltpu.make_async_copy(gout, gall.at[me], lsem.at[0])
    own.start()
    greet(
        [
            device(x, (y + 1) % NY, z, c), device(x, (y + NY - 1) % NY, z, c),
            device(x, y, (z + 1) % NZ, c), device(x, y, (z + NZ - 1) % NZ, c),
        ]
    )
    own.wait()
    pos = (x, y, z)

    def finish(kv):
        def done(value):
            sums[kv] = value

        return done

    def term(kv):
        return lambda py, pz: acc.at[py * NZ + pz, kv]

    def piece(t):
        return lambda py, pz: gall.at[py * NZ + pz, t]

    def half(t):
        return lambda py, pz, h: gall.at[py * NZ + pz, t, h]

    nothing = lambda py, pz: None
    some = [gall.at[pl.ds(0, PLANE - 1), t] for t in range(2)]
    play(
        reduce_flow(term(0), got_k, out_k, ("z", "y"), pos, c, (k_ssem, k_rsem), finish(0), 32),
        reduce_flow(term(1), got_v, out_v, ("y", "z"), pos, c, (v_ssem, v_rsem), finish(1), 32),
        gather_flow(piece(0), half(0), ("y", "z"), pos, c, (o_ssem, o_rsem), nothing, 8, some[0]),
        gather_flow(piece(1), half(1), ("z", "y"), pos, c, (w_ssem, w_rsem), nothing, 8, some[1]),
    )


def kernel_d(glob, sums, near_sum, att_in, dq_in, gall, att, dq, dk, dv):
    shard = lax.axis_index("pb") * 8 + lax.axis_index("ka")
    dk[...] = (sums[0] + near_sum[0]).astype(BF16)
    dv[...] = (sums[1] + near_sum[1]).astype(BF16)
    for j in range(2):
        blocks = jnp.full((16, HD), shard * 2 + j, jnp.int32)
        is_glob = [blocks == glob[g] for g in range(2)]
        for t, src, dst in ((0, att_in, att), (1, dq_in, dq)):
            for p in range(PLANE):
                cols = slice((p // 4) * HD, (p // 4 + 1) * HD)
                value = jnp.where(is_glob[1], gall[p, t, 1], src[j, p % 4, :, cols])
                dst[j, p % 4, :, cols] = jnp.where(is_glob[0], gall[p, t, 0], value)


def body(queries, key_vectors, value_vectors, out_grad, rand_blocks, global_blocks):
    vmem = pl.BlockSpec(memory_space=pltpu.VMEM)
    smem = pl.BlockSpec(memory_space=pltpu.SMEM)
    hbm = pl.BlockSpec(memory_space=pl.ANY)
    off = pl.BlockSpec(memory_space=pltpu.HBM)
    shape = jax.ShapeDtypeStruct
    dma = pltpu.SemaphoreType.DMA
    rows = (2, 4, 16, HEADS * HD)
    rand = rand_blocks.T
    yz, zy = ("y", "z"), ("z", "y")
    ga, gb = GATHER_SEMS[yz], GATHER_SEMS[zy]
    mk, mv = REDUCE_MSGS[zy], REDUCE_MSGS[yz]
    att, dq, contrib, dense, near_sum, gout, rand_sib = pl.pallas_call(
        kernel_a,
        name="exchange_and_attend",
        out_shape=(
            shape(rows, BF16),
            shape(rows, BF16),
            shape((8, SLOTS + 2, 2, BLOCK, HD), BF16),
            shape((PLANE, 2, HD, HD), F32),
            shape((2, HD, HD), F32),
            shape((2, 2, 16, HD), BF16),
            shape((3, 16), jnp.int32),
        ),
        in_specs=[off] * 6,
        out_specs=(vmem, vmem, vmem, vmem, vmem, vmem, hbm),
        scratch_shapes=[
            pltpu.VMEM((2, PLANE, 2, 2, BLOCK, HD), BF16),
            pltpu.VMEM((PLANE, 64, HD), BF16),
            pltpu.VMEM((mv, 64, HD), BF16),
            pltpu.VMEM((mv, 64, HD), BF16),
            pltpu.VMEM((8, 2, 2, 16, HD), BF16),
            pltpu.VMEM((2, 2, 4, 2, BLOCK, HD), BF16),
            pltpu.VMEM((2, 13, 2, BLOCK, HD), BF16),
            pltpu.VMEM((3, 9, 2, BLOCK, HD), BF16),
            pltpu.VMEM((8, 32, HD), F32),
            pltpu.VMEM((8, 2, 32, HD), F32),
            pltpu.SMEM((3, 16), jnp.int32),
            pltpu.SMEM((2,), jnp.int32),
            pltpu.VMEM(rows, BF16),
            pltpu.VMEM(rows, BF16),
            pltpu.VMEM((32, PLANE * HD), F32),
            pltpu.VMEM((32, PLANE * HD), F32),
            pltpu.VMEM((32, PLANE * HD), BF16),
            pltpu.VMEM((32, PLANE * HD), BF16),
            pltpu.VMEM((32, HD), BF16),
            pltpu.VMEM((32, HD), BF16),
            pltpu.VMEM((512, HD), BF16),
            pltpu.VMEM((512, HD), BF16),
            pltpu.VMEM((1024, HD), BF16),
            pltpu.VMEM((1024, HD), BF16),
            pltpu.VMEM((2, 512, HD), F32),
            pltpu.VMEM((4, HD, HD), F32),
            dma((1,)), dma((ga,)), dma((1,)), dma((gb,)), dma((1,)), dma((mv,)),
            dma((8,)), dma((8,)), dma((6,)), dma((6,)), dma((12,)), dma((12,)), dma((6,)),
        ],
        compiler_params=pltpu.CompilerParams(
            collective_id=0, has_side_effects=True, vmem_limit_bytes=VMEM_A
        ),
    )(
        rand, global_blocks, queries.reshape(rows),
        key_vectors.reshape(2, BLOCK, HD), value_vectors.reshape(2, BLOCK, HD), out_grad.reshape(rows),
    )
    acc = pl.pallas_call(
        kernel_b,
        name="spread_terms",
        out_shape=shape((PLANE, 2, HD, HD), F32),
        in_specs=[smem, smem, smem, vmem, vmem],
        out_specs=vmem,
        input_output_aliases={4: 0},
        compiler_params=pltpu.CompilerParams(vmem_limit_bytes=VMEM_B),
    )(rand, rand_sib, global_blocks, contrib, dense)
    sums, gall = pl.pallas_call(
        kernel_c,
        name="reduce_and_gather",
        out_shape=(shape((2, HD, HD), F32), shape((PLANE, 2, 2, 16, HD), BF16)),
        in_specs=[vmem] * 2,
        out_specs=(vmem,) * 2,
        scratch_shapes=[
            pltpu.VMEM((mk, HD, HD), BF16), pltpu.VMEM((mk, HD, HD), BF16),
            pltpu.VMEM((mv, HD, HD), BF16), pltpu.VMEM((mv, HD, HD), BF16),
            dma((1,)), dma((mk,)), dma((1,)), dma((mv,)),
            dma((1,)), dma((ga,)), dma((1,)), dma((gb,)), dma((1,)),
        ],
        compiler_params=pltpu.CompilerParams(
            collective_id=1, has_side_effects=True, vmem_limit_bytes=VMEM_C
        ),
    )(acc, gout)
    att, dq, dk, dv = pl.pallas_call(
        kernel_d,
        name="finish",
        out_shape=(shape(rows, BF16), shape(rows, BF16), shape((HD, HD), BF16), shape((HD, HD), BF16)),
        in_specs=[smem] + [vmem] * 5,
        out_specs=(vmem,) * 4,
        compiler_params=pltpu.CompilerParams(vmem_limit_bytes=VMEM_D),
    )(global_blocks, sums, near_sum, att, dq, gall)
    return att.reshape(queries.shape), dq.reshape(queries.shape), dk, dv


def solution(mesh):
    assert (mesh.shape["pb"], mesh.shape["ka"]) == (32, 8)
    rows = P(("pb", "ka"), None)
    return jax.shard_map(
        body,
        mesh=mesh,
        in_specs=(rows, rows, rows, rows, P("pb", None), P()),
        out_specs=(rows, rows, rows, rows),
        check_vma=False,
    )
```

```python
import math

import jax
import jax.numpy as jnp
from jax import lax
from jax.experimental import pallas as pl
from jax.experimental.pallas import tpu as pltpu
from jax.sharding import PartitionSpec as P

NX, NY, NZ = 4, 4, 8
PLANE = NY * NZ
SHARDS = 256
NBLK = 512
BLOCK = 64
HD = 128
HEADS = 8
SLOTS = 8
SCALE = 1.0 / math.sqrt(HD)
NEG = -1e30
VMEM_A, VMEM_B, VMEM_C, VMEM_D = 28 << 20, 14 << 20, 14 << 20, 8 << 20
MESH = pl.DeviceIdType.MESH
F32, BF16 = jnp.float32, jnp.bfloat16


def here():
    pb, ka = lax.axis_index("pb"), lax.axis_index("ka")
    return ka % 4, pb // 8, (ka // 4) * 4 + (pb // 2) % 4, pb % 2


def device(x, y, z, c):
    return ((y * 4 + z % 4) * 2 + c, (z // 4) * 4 + x)


def place(block):
    shard = block // 2
    pb, ka = shard // 8, shard % 8
    return ka % 4, pb % 2, (pb // 8) * 8 + (ka // 4) * 4 + (pb // 2) % 4, block % 2


def remote(src, dst, ssem, rsem, dev):
    return pltpu.make_async_remote_copy(
        src_ref=src, dst_ref=dst, send_sem=ssem, recv_sem=rsem, device_id=dev, device_id_type=MESH
    )


RATE, CORE_RATE, LATENCY, AHEAD, FAVOUR = 50.0, 200.0, 1.6, 2.0, 0


def schedule(msgs, favoured=()):
    depth, changed = [1] * len(msgs), True
    while changed:
        changed = False
        for i in range(len(msgs) - 1, -1, -1):
            for dep in msgs[i][0]:
                if depth[dep] <= depth[i]:
                    depth[dep], changed = depth[i] + 1, True
    ranked = sorted(range(len(msgs)), key=lambda i: (-depth[i] - (FAVOUR if i in favoured else 0), i))
    now, free, arrival, come, order = 0.0, {}, {}, set(), []
    while len(come) < len(msgs):
        for i in ranked:
            deps, link, size, work = msgs[i][:4]
            begin = now if link is None else max(free.get(link, 0.0), now)
            if i in arrival or begin > now + AHEAD or any(dep not in come for dep in deps):
                continue
            now += work
            if link is None:
                arrival[i] = now + size
            else:
                free[link] = max(begin, now) + size / (CORE_RATE if link == "core" else RATE)
                arrival[i] = free[link] + LATENCY
            order.append(("send", i))
        i = min((i for i in arrival if i not in come), key=lambda i: (arrival[i], i))
        now = max(now, arrival[i]) + 0.05
        come.add(i)
        order.append(("wait", i))
    return order


def play(flows, more=None, after=None, favour=None):
    msgs, members = [], []
    for own, end in flows:
        base = len(msgs)
        members.append(list(range(base, base + len(own))))
        msgs += [([dep + base for dep in m[0]],) + m[1:] for m in own]
    first = len(msgs)
    if after is not None:
        msgs = [(m[0] or after(first),) + m[1:] for m in msgs]
    if more is not None:
        msgs += more(members)
    for what, i in schedule(msgs, () if favour is None else members[favour]):
        msgs[i][4 if what == "send" else 5]()
    for own, end in flows:
        end()


def ring_around(order, pos, core):
    x, y, z = pos

    def at(o1, o2):
        oy, oz = (o1, o2) if order[0] == "y" else (o2, o1)
        return (y + oy + NY) % NY, (z + oz + NZ) % NZ

    def dev(axis, d):
        step = 1 if d == 0 else -1
        if axis == "y":
            return device(x, (y + step + NY) % NY, z, core)
        return device(x, y, (z + step + NZ) % NZ, core)

    return at, dev, RING[order[0]], RING[order[1]]


RING = {"y": NY, "z": NZ}


def gather_flow(piece, half, order, pos, core, sems, arrived, kb, whole):
    ssem, rsem = sems
    at, dev, n1, n2 = ring_around(order, pos, core)
    msgs, index, seen = [], {}, {}

    def message(deps, o1, o2, nxt, d, halved, axis):
        i = len(msgs)

        def copy(a, b):
            cy, cz = at(a, b)
            ref = half(cy, cz, d) if halved else piece(cy, cz)
            return remote(ref, ref, ssem.at[0], rsem.at[i], dev(axis, d))

        def send():
            copy(o1, o2).start()

        def wait():
            copy(*nxt).wait_recv()
            spot = tuple(abs(o) if abs(o) == n // 2 else o for o, n in zip(nxt, (n1, n2)))
            seen[spot] = seen.get(spot, 0) + 1
            if seen[spot] == (2 if halved else 1):
                arrived(*at(*nxt))

        msgs.append((deps, (axis, d), kb / 2 if halved else kb, 0.02, send, wait))
        return i

    for k in range(n1 // 2):
        for d in (0, 1):
            sign = -1 if d == 0 else 1
            deps = [index[1, sign * k, d]] if k else []
            i = message(deps, sign * k, 0, (sign * (k + 1), 0), d, k == n1 // 2 - 1, order[0])
            index[1, sign * (k + 1), d] = i
    offsets = [0] + [s * k for k in range(1, n1 // 2) for s in (-1, 1)] + [n1 // 2]
    for o in offsets:
        if o == 0:
            first = []
        elif o == n1 // 2:
            first = [index[1, -o, 0], index[1, o, 1]]
        else:
            first = [index[1, o, 0 if o < 0 else 1]]
        for k in range(n2 // 2):
            for d in (0, 1):
                sign = -1 if d == 0 else 1
                deps = [index[2, o, sign * k, d]] if k else first
                i = message(deps, o, sign * k, (o, sign * (k + 1)), d, k == n2 // 2 - 1, order[1])
                index[2, o, sign * (k + 1), d] = i

    def end():
        remote(whole, whole, ssem.at[0], rsem.at[0], dev("y", 0)).wait_send()

    return msgs, end


GATHER_SEMS = {("y", "z"): NY + NY * NZ, ("z", "y"): NZ + NZ * NY}


def reduce_flow(own, got, out, order, pos, core, sems, done, kb):
    ssem, rsem = sems
    at, dev, n1, n2 = ring_around(order, pos, core)
    rows = got.shape[1] // 2
    msgs = []

    def half_of(ref, d):
        return ref.at[pl.ds(d * rows, rows)]

    def load(ref, h):
        return (ref[...] if h is None else half_of(ref, h)[...]).astype(F32)

    def ring(n, axis, term, deps_of):
        steps = n // 2
        base = len(msgs)
        for d in (0, 1):
            for t in range(steps):
                o = (1 if d == 0 else -1) * (steps - t)
                i = base + d * steps + t
                deps = list(deps_of(o)) + ([i - 1] if t else [])

                def copy(i=i, t=t, d=d):
                    src, dst = out.at[i], got.at[i]
                    if t == 0:
                        src, dst = half_of(src, d), half_of(dst, d)
                    return remote(src, dst, ssem.at[0], rsem.at[i], dev(axis, d))

                def send(i=i, o=o, t=t, d=d, copy=copy):
                    value = term(o)
                    if t == 0:
                        half_of(out.at[i], d)[...] = value(d).astype(BF16)
                    elif t == 1:
                        half_of(out.at[i], d)[...] = (value(d) + load(got.at[i - 1], d)).astype(BF16)
                        half_of(out.at[i], 1 - d)[...] = value(1 - d).astype(BF16)
                    else:
                        out[i] = (value(None) + load(got.at[i - 1], None)).astype(BF16)
                    copy().start()

                def wait(copy=copy):
                    copy().wait_recv()

                msgs.append((deps, (axis, d), kb if t else kb / 2, 0.005 * kb, send, wait))
        return base

    offsets = [n2 // 2] + [s * k for k in range(n2 // 2 - 1, 0, -1) for s in (-1, 1)] + [0]
    ends = {}
    for o2 in offsets:

        def term(o1, o2=o2):
            ref = own(*at(o1, o2))
            return lambda h: load(ref, h)

        base = ring(n1, order[0], term, lambda o: [])
        ends[o2] = (base + n1 // 2 - 1, base + n1 - 1)
    ends[-(n2 // 2)] = ends[n2 // 2]

    def term2(o2):
        a, b = ends[o2]
        ref = own(*at(0, o2))
        return lambda h: load(ref, h) + load(got.at[a], h) + load(got.at[b], h)

    base = ring(n2, order[1], term2, lambda o: ends[o])

    def result():
        last = (base + n2 // 2 - 1, base + n2 - 1)
        return term2(0)(None) + load(got.at[last[0]], None) + load(got.at[last[1]], None)

    def end():
        if done is not None:
            done(result())
        whole = out.at[pl.ds(0, PLANE - 1)]
        remote(whole, whole, ssem.at[0], rsem.at[0], dev("y", 0)).wait_send()

    return (msgs, end), result


REDUCE_MSGS = {("y", "z"): NY * NZ + NZ, ("z", "y"): NZ * NY + NY}


def greet(devices):
    barrier = pltpu.get_barrier_semaphore()
    for dev in devices:
        pl.semaphore_signal(barrier, inc=1, device_id=dev, device_id_type=MESH)
    pl.semaphore_wait(barrier, len(devices))


def nt(a, b):
    return lax.dot_general(a, b, (((1,), (1,)), ((), ())), preferred_element_type=F32)


def tn(a, b):
    return lax.dot_general(a, b, (((0,), (0,)), ((), ())), preferred_element_type=F32)


def nn(a, b):
    return lax.dot_general(a, b, (((1,), (0,)), ((), ())), preferred_element_type=F32)


def kernel_a(
    rand_any, glob_any, q_any, k, v, d_any,
    att, dq, contrib, dense, near_sum, gout, rand_sib,
    col_k, col_v, gown, g_got, g_out_buf, sel, xm_a, xm_b, xm_c, xm_d, xs, xall, stat, part,
    rand, glob, q, d, sg, dpg, gp, gs, gq, gd, kc, vc, qs, ds_, dkv, own_sum,
    a_ssem, a_rsem, b_ssem, b_rsem, g_ssem, g_rsem, c_ssem, c_rsem, x_ssem, x_rsem, ssem, rsem, lsem,
):
    x, y, z, c = here()
    col, xm = (col_k, col_v), ((xm_a, xm_b), (xm_c, xm_d))
    pb, ka = lax.axis_index("pb"), lax.axis_index("ka")
    shard = pb * 8 + ka
    me = y * NZ + z
    row = c * 4 + x
    zh = z // 4
    pos = (x, y, z)

    def row_dev(r):
        return device(r % 4, y, z, r // 4)

    def x_dev(step):
        return device((x + step + 4) % 4, y, z, c)

    row_peers = [(row + i) % 8 for i in range(1, 8)]
    sibling = row_dev((row + 4) % 8)

    local = [
        pltpu.make_async_copy(k, col[0].at[c, me], lsem.at[0]),
        pltpu.make_async_copy(v, col[1].at[c, me], lsem.at[1]),
        pltpu.make_async_copy(q_any, q, lsem.at[2]),
        pltpu.make_async_copy(d_any, d, lsem.at[3]),
        pltpu.make_async_copy(rand_any, rand, lsem.at[4]),
        pltpu.make_async_copy(glob_any, glob, lsem.at[5]),
    ]
    for cp in local:
        cp.start()
    greet(
        [
            device(x, (y + 1) % NY, z, c), device(x, (y + NY - 1) % NY, z, c),
            device(x, y, (z + 1) % NZ, c), device(x, y, (z + NZ - 1) % NZ, c),
        ]
        + [row_dev(r) for r in row_peers]
    )
    for cp in local:
        cp.wait()
    rand_copy = remote(rand_any, rand_sib, ssem.at[2], rsem.at[2], sibling)
    rand_copy.start()

    def pass_on(kv):
        def arrived(py, pz):
            ref = col[kv].at[c, py * NZ + pz]
            remote(ref, ref, ssem.at[3 + kv], rsem.at[3 + kv], sibling).start()

        return arrived

    def piece(kv):
        return lambda py, pz: col[kv].at[c, py * NZ + pz]

    def half(kv):
        return lambda py, pz, h: col[kv].at[c, py * NZ + pz, h]

    def some(kv):
        return col[kv].at[0, pl.ds(0, PLANE - 1)]

    flow_k = gather_flow(
        piece(0), half(0), ("y", "z"), pos, c, (a_ssem, a_rsem), pass_on(0), 32, some(0)
    )
    flow_v = gather_flow(
        piece(1), half(1), ("z", "y"), pos, c, (b_ssem, b_rsem), pass_on(1), 32, some(1)
    )
    pass_on(0)(y, z)
    pass_on(1)(y, z)

    g_place = [place(glob[g]) for g in range(2)]
    shards = jnp.full((16, HD), shard, jnp.int32)
    for g in range(2):
        mine = shards == glob[g] // 2
        for t, ref in ((0, q), (1, d)):
            for p in range(PLANE):
                value = ref[g_place[g][3], p % 4, :, (p // 4) * HD : (p // 4 + 1) * HD]
                rows = slice((g * 2 + t) * 16, (g * 2 + t + 1) * 16)
                gown[p, rows, :] = jnp.where(mine, value, jnp.zeros_like(value))

    flow_g, tiles = reduce_flow(
        lambda py, pz: gown.at[py * NZ + pz], g_got, g_out_buf, ("y", "z"), pos, c, (g_ssem, g_rsem),
        None, 16,
    )

    for j in range(2):
        for h in range(HEADS):
            rows = pl.ds(j * 512 + h * 64, 64)
            qs[rows, :] = q[j, :, :, h * HD : (h + 1) * HD].reshape(64, HD)
            ds_[rows, :] = d[j, :, :, h * HD : (h + 1) * HD].reshape(64, HD)

    def send_sel():
        sel[row] = tiles().reshape(2, 2, 16, HD).astype(BF16)
        for r in row_peers:
            remote(sel.at[row], sel.at[row], ssem.at[6], rsem.at[6], row_dev(r)).start()

    def wait_sel():
        remote(sel.at[pl.ds(0, 7)], sel.at[pl.ds(0, 7)], ssem.at[6], rsem.at[6], sibling).wait_recv()

    def wanted(ka_of, slot):
        if slot >= 6:
            return glob[slot - 6]
        return rand[slot % 3, ka_of * 2 + slot // 3]

    def ka_at(step):
        return zh * 4 + (x + step + 4) % 4

    def slot_at(direction, i):
        return i if direction == 0 else (i + 4) % 8

    def block_of(kv, block):
        bx, bc, bp, bh = place(block)
        return col[kv][bc, bp, bh]

    def x_copy(kv, dr, kind):
        src, dst = (
            (xs.at[kv, dr, pl.ds(9, 4)], xm[kv][dr].at[0]),
            (xs.at[kv, dr, pl.ds(4, 5)], xall.at[kv, dr, pl.ds(4, 5)]),
            (xs.at[kv, dr, pl.ds(0, 4)], xall.at[kv, dr, pl.ds(0, 4)]),
        )[kind]
        sem = kv * 6 + dr * 3 + kind
        return remote(src, dst, x_ssem.at[sem], x_rsem.at[sem], x_dev(1 - 2 * dr))

    def column_in(kv):
        ref = col[kv].at[1 - c]
        remote(ref, ref, ssem.at[3 + kv], rsem.at[3 + kv], sibling).wait_recv()

    def send_far(kv, dr):
        for i in range(4):
            xs[kv, dr, 9 + i] = block_of(kv, wanted(ka_at(2), slot_at(dr, i)))
        x_copy(kv, dr, 0).start()

    def send_near(kv, dr):
        step = 1 - 2 * dr
        for i in range(4, 8):
            xs[kv, dr, i] = block_of(kv, wanted(ka_at(step), slot_at(dr, i)))
        to = pb * 8 + ka_at(step)
        edge = (to * 2 + 2 * SHARDS - 1) % NBLK if dr == 0 else (to * 2 + 2) % NBLK
        xs[kv, dr, 8] = block_of(kv, edge)
        x_copy(kv, dr, 1).start()
        for i in range(4):
            xm[kv][dr][1, i] = block_of(kv, wanted(ka_at(step), slot_at(dr, i)))
        for i in range(4):
            xall[kv, 2, dr * 4 + i] = block_of(kv, wanted(ka, dr * 4 + i))

    def send_merged(kv, dr):
        for i in range(4):
            bx = place(wanted(ka_at(1 - 2 * dr), slot_at(dr, i)))[0]
            xs[kv, dr, i] = xm[kv][dr][jnp.where(bx == x, 1, 0), i]
        x_copy(kv, dr, 2).start()

    def global_scores():
        for g in range(2):
            gx, gc, gpl, gh = g_place[g]
            gq[pl.ds(g * 16, 16), :] = sel[gc * 4 + gx, g, 0]
            gd[pl.ds(g * 16, 16), :] = sel[gc * 4 + gx, g, 1]
        for i in range(4):
            lanes, ps = slice(i * 1024, (i + 1) * 1024), pl.ds(i * 8, 8)
            sg[:, lanes] = nt(gq[...], col[0][c, ps].reshape(1024, HD)) * SCALE
            dpg[:, lanes] = nt(gd[...], col[1][c, ps].reshape(1024, HD))
        g_max = jnp.max(sg[...], axis=1, keepdims=True)
        g_exp = jnp.exp(sg[...] - g_max)
        g_sum = jnp.sum(g_exp, axis=1, keepdims=True)
        g_dot = jnp.sum(g_exp * dpg[...], axis=1, keepdims=True)
        lane = lax.broadcasted_iota(jnp.int32, (32, HD), 1)
        stat[row] = jnp.where(lane == 0, g_max, jnp.where(lane == 1, g_sum, g_dot))
        for r in row_peers:
            remote(stat.at[row], stat.at[row], ssem.at[8], rsem.at[8], row_dev(r)).start()

    nothing = lambda: None

    def exchange(members):
        keys, values, rows_g = members
        n = len(keys) + len(values) + len(rows_g)
        more = [(rows_g, None, 2.5, 0.1, send_sel, wait_sel)]
        for kv, flow in ((0, keys), (1, values)):
            here_in = n + len(more)
            more.append((flow, None, 1.6, 0.0, nothing, lambda kv=kv: column_in(kv)))
            far = n + len(more)
            for kind, send, deps, kb in (
                (0, send_far, lambda dr: [here_in], 64),
                (1, send_near, lambda dr: [here_in], 80),
                (2, send_merged, lambda dr: [here_in, far + dr, far + 2 + dr], 64),
            ):
                for dr in range(2):
                    more.append(
                        (
                            deps(dr), ("x", dr), kb, 0.2,
                            lambda kv=kv, dr=dr, send=send: send(kv, dr),
                            lambda kv=kv, dr=dr, kind=kind: x_copy(kv, dr, kind).wait_recv(),
                        )
                    )
        more.append((keys + values + [n], None, 0.1, 1.5, global_scores, nothing))
        return more

    play((flow_k, flow_v, flow_g), exchange, favour=0)

    slot_of = lax.broadcasted_iota(jnp.int32, (1, 512), 1) // BLOCK
    for j in range(2):
        block = shard * 2 + j
        cand = [block - 1, block, block + 1, glob[0], glob[1]]
        cand += [rand[r, ka * 2 + j] for r in range(3)]
        for kv, dst in ((0, kc), (1, vc)):
            near_refs = [xall.at[kv, 0, 8], col[kv].at[c, me, 0], col[kv].at[c, me, 1], xall.at[kv, 1, 8]]
            for i in range(3):
                dst[i * BLOCK : (i + 1) * BLOCK, :] = near_refs[i + j][...]
            for i in range(3, 8):
                slot = 6 + i - 3 if i < 5 else j * 3 + i - 5
                far = 0 if slot < 4 else 1
                off = (place(cand[i])[0] + 4 - x) % 4
                src = jnp.where(off == 0, 2, jnp.where(off == 3, 0, jnp.where(off == 1, 1, far)))
                spot = jnp.where(src == 1, (slot + 4) % 8, slot)
                dst[i * BLOCK : (i + 1) * BLOCK, :] = xall[kv, src, spot]
        cands = jnp.zeros((1, 512), jnp.int32)
        for i in range(8):
            cands = jnp.where(slot_of == i, cand[i], cands)
        out = (cands < 0) | (cands >= NBLK)
        for i in range(7):
            out = out | ((slot_of > i) & (cands == cand[i]))
        bias = jnp.where(out, NEG, 0.0)
        blocks = jnp.full((256, 1), block, jnp.int32)
        keep = jnp.where((blocks == glob[0]) | (blocks == glob[1]), 0.0, 1.0)
        for part_i in range(2):
            rows = pl.ds(j * 512 + part_i * 256, 256)
            qv, dv = qs[rows, :], ds_[rows, :]
            s = nt(qv, kc[...]) * SCALE + bias
            e = jnp.exp(s - jnp.max(s, axis=1, keepdims=True))
            w = e * (keep / jnp.sum(e, axis=1, keepdims=True))
            wb = w.astype(BF16)
            o = nn(wb, vc[...]).astype(BF16)
            dot = jnp.sum(dv.astype(F32) * o.astype(F32), axis=1, keepdims=True)
            ds = (w * (nt(dv, vc[...]) - dot)).astype(BF16)
            dqv = (nn(ds, kc[...]) * SCALE).astype(BF16)
            for h in range(4):
                cols = slice((part_i * 4 + h) * HD, (part_i * 4 + h + 1) * HD)
                att[j, :, :, cols] = o[h * 64 : (h + 1) * 64].reshape(4, 16, HD)
                dq[j, :, :, cols] = dqv[h * 64 : (h + 1) * 64].reshape(4, 16, HD)
            dk_new, dv_new = tn(ds, qv) * SCALE, tn(wb, dv)
            if part_i == 0:
                dkv[0], dkv[1] = dk_new, dv_new
            else:
                dkv[0] += dk_new
                dkv[1] += dv_new
        for kv in range(2):
            for i in range(8):
                term = dkv[kv, i * BLOCK : (i + 1) * BLOCK, :]
                spot = i + j - 1
                if i < 3 and spot in (-1, 2):
                    contrib[row, 9 if spot == -1 else 0, kv] = term.astype(BF16)
                elif i < 3:
                    if (j, i) in ((0, 1), (0, 2)):
                        own_sum[kv, pl.ds(spot * BLOCK, BLOCK), :] = term
                    else:
                        total = own_sum[kv, pl.ds(spot * BLOCK, BLOCK), :] + term
                        near_sum[kv, pl.ds(spot * BLOCK, BLOCK), :] = total
                elif i >= 5:
                    contrib[row, 1 + j * 3 + i - 5, kv] = term.astype(BF16)
                elif j == 0:
                    own_sum[2 + kv, pl.ds((i - 3) * BLOCK, BLOCK), :] = term
                else:
                    total = own_sum[2 + kv, pl.ds((i - 3) * BLOCK, BLOCK), :] + term
                    contrib[row, 7 + i - 3, kv] = total.astype(BF16)

    def c_copy(src, first, n, step, sem):
        ref = contrib.at[src, pl.ds(first, n)]
        dev = sibling if step is None else x_dev(step)
        return remote(ref, ref, c_ssem.at[sem], c_rsem.at[sem], dev)

    def at_x(o):
        return c * 4 + (x + o + 4) % 4

    c_sends = [c_copy(row, 0, 9, 1, 0), c_copy(row, 1, 9, -1, 1), c_copy(row, 1, 8, None, 4)]
    for cp in c_sends:
        cp.start()

    remote(stat.at[pl.ds(0, 7)], stat.at[pl.ds(0, 7)], ssem.at[8], rsem.at[8], sibling).wait_recv()
    stats = [stat[i] for i in range(8)]
    top = stats[0][:, 0:1]
    for i in range(1, 8):
        top = jnp.maximum(top, stats[i][:, 0:1])
    total, dot = jnp.zeros((32, 1), F32), jnp.zeros((32, 1), F32)
    for i in range(8):
        f = jnp.exp(stats[i][:, 0:1] - top)
        total += stats[i][:, 1:2] * f
        dot += stats[i][:, 2:3] * f
    g_row = lax.broadcasted_iota(jnp.int32, (32, 1), 0)
    g_one = jnp.full((32, 1), glob[1], jnp.int32)
    first = jnp.where((g_row >= 16) & (g_one == glob[0]), 0.0, 1.0)
    gw = jnp.exp(sg[...] - top) * (first / total)
    gp[...] = gw.astype(BF16)
    gs[...] = (gw * (dpg[...] - dot / total)).astype(BF16)
    g_o, g_dq = jnp.zeros((32, HD), F32), jnp.zeros((32, HD), F32)
    for i in range(4):
        lanes, ps = slice(i * 1024, (i + 1) * 1024), pl.ds(i * 8, 8)
        g_o += nn(gp[:, lanes], col[1][c, ps].reshape(1024, HD))
        g_dq += nn(gs[:, lanes], col[0][c, ps].reshape(1024, HD))
    part[row, 0] = g_o
    part[row, 1] = g_dq * SCALE
    for r in row_peers:
        remote(part.at[row], part.at[row], ssem.at[11], rsem.at[11], row_dev(r)).start()

    c_copy(at_x(-1), 0, 9, 1, 0).wait_recv()
    more = [c_copy(at_x(-1), 1, 4, 1, 2), c_copy(at_x(-1), 0, 9, None, 5)]
    for cp in more:
        cp.start()
    c_copy(at_x(1), 1, 9, -1, 1).wait_recv()
    more += [c_copy(at_x(1), 5, 4, -1, 3), c_copy(at_x(1), 1, 9, None, 6)]
    for cp in more[2:]:
        cp.start()
    c_sends += more

    for i in range(4):
        lanes, ps = slice(i * 1024, (i + 1) * 1024), pl.ds(i * 8, 8)
        dense[ps, 0] = (tn(gs[:, lanes], gq[...]) * SCALE).reshape(8, HD, HD)
        dense[ps, 1] = tn(gp[:, lanes], gd[...]).reshape(8, HD, HD)

    c_copy(at_x(2), 1, 4, 1, 2).wait_recv()
    c_copy(at_x(2), 5, 4, -1, 3).wait_recv()
    last = c_copy(at_x(2), 1, 8, None, 7)
    last.start()
    c_sends.append(last)

    remote(part.at[pl.ds(0, 7)], part.at[pl.ds(0, 7)], ssem.at[11], rsem.at[11], sibling).wait_recv()
    for t in range(2):
        acc = part[0, t]
        for i in range(1, 8):
            acc += part[i, t]
        for g in range(2):
            gout[t, g] = acc[g * 16 : (g + 1) * 16].astype(BF16)

    def at_other(o):
        return (1 - c) * 4 + (x + o + 4) % 4

    for sem, o, first, n in ((4, 0, 1, 8), (5, -1, 0, 9), (6, 1, 1, 9), (7, 2, 1, 8)):
        c_copy(at_other(o), first, n, None, sem).wait_recv()
    rand_copy.wait_recv()

    for cp in c_sends + [rand_copy]:
        cp.wait_send()
    for kv in range(2):
        remote(col[kv].at[c], col[kv].at[c], ssem.at[3 + kv], rsem.at[3 + kv], sibling).wait_send()
    for ref, sem in ((sel, 6), (stat, 8), (part, 11)):
        remote(ref.at[pl.ds(0, 7)], ref.at[pl.ds(0, 7)], ssem.at[sem], rsem.at[sem], sibling).wait_send()
    for kv in range(2):
        for dr in range(2):
            for kind in range(3):
                x_copy(kv, dr, kind).wait_send()


def kernel_b(rand_any, rand_sib, glob_any, contrib, dense, acc, rand, glob, sem):
    x, y, z, c = here()
    zh = z // 4
    del dense
    copies = [
        pltpu.make_async_copy(rand_any, rand, sem.at[0]),
        pltpu.make_async_copy(glob_any, glob, sem.at[1]),
    ]
    for cp in copies:
        cp.start()
    for cp in copies:
        cp.wait()

    def add(block, here_too, src, entry):
        bx, bc, bp, bh = place(block)

        @pl.when(here_too & (bx == x) & (bc == c))
        def _():
            rows = pl.ds(pl.multiple_of(bh * BLOCK, BLOCK), BLOCK)
            acc[bp, :, rows, :] += contrib[src, entry].astype(F32)

    for core in range(2):
        for xs in range(NX):
            src = core * 4 + xs
            shard = ((y * 4 + z % 4) * 2 + core) * 8 + zh * 4 + xs
            for slot in range(SLOTS):
                if slot >= 6:
                    block = glob[slot - 6]
                else:
                    r, s = (zh * 4 + xs) * 2 + slot // 3, slot % 3
                    block = jnp.where(c == core, rand[s, r], rand_sib[s, r])
                add(block, True, src, 1 + slot)
            after, before = shard * 2 + 2, shard * 2 - 1
            add(jnp.minimum(after, NBLK - 1), (after < NBLK) & ((xs - x + 4) % 4 == 3), src, 0)
            add(jnp.maximum(before, 0), (before >= 0) & ((xs - x + 4) % 4 == 1), src, 9)


def kernel_c(
    acc, gout,
    sums, gall,
    got_k, out_k, got_v, out_v,
    k_ssem, k_rsem, v_ssem, v_rsem, o_ssem, o_rsem, w_ssem, w_rsem, lsem,
):
    x, y, z, c = here()
    me = y * NZ + z
    own = pltpu.make_async_copy(gout, gall.at[me], lsem.at[0])
    own.start()
    greet(
        [
            device(x, (y + 1) % NY, z, c), device(x, (y + NY - 1) % NY, z, c),
            device(x, y, (z + 1) % NZ, c), device(x, y, (z + NZ - 1) % NZ, c),
        ]
    )
    own.wait()
    pos = (x, y, z)

    def finish(kv):
        def done(value):
            sums[kv] = value

        return done

    def term(kv):
        return lambda py, pz: acc.at[py * NZ + pz, kv]

    def piece(t):
        return lambda py, pz: gall.at[py * NZ + pz, t]

    def half(t):
        return lambda py, pz, h: gall.at[py * NZ + pz, t, h]

    nothing = lambda py, pz: None
    some = [gall.at[pl.ds(0, PLANE - 1), t] for t in range(2)]
    play(
        (
            reduce_flow(term(0), got_k, out_k, ("z", "y"), pos, c, (k_ssem, k_rsem), finish(0), 32)[0],
            reduce_flow(term(1), got_v, out_v, ("y", "z"), pos, c, (v_ssem, v_rsem), finish(1), 32)[0],
            gather_flow(piece(0), half(0), ("y", "z"), pos, c, (o_ssem, o_rsem), nothing, 8, some[0]),
            gather_flow(piece(1), half(1), ("z", "y"), pos, c, (w_ssem, w_rsem), nothing, 8, some[1]),
        )
    )


def kernel_d(glob_any, sums, near_sum, att_in, dq_in, gall, att, dq, dk, dv, glob, sem):
    cp = pltpu.make_async_copy(glob_any, glob, sem.at[0])
    cp.start()
    shard = lax.axis_index("pb") * 8 + lax.axis_index("ka")
    dk[...] = (sums[0] + near_sum[0]).astype(BF16)
    dv[...] = (sums[1] + near_sum[1]).astype(BF16)
    cp.wait()
    for j in range(2):
        blocks = jnp.full((16, HD), shard * 2 + j, jnp.int32)
        is_glob = [blocks == glob[g] for g in range(2)]
        for t, src, dst in ((0, att_in, att), (1, dq_in, dq)):
            for p in range(PLANE):
                cols = slice((p // 4) * HD, (p // 4 + 1) * HD)
                value = jnp.where(is_glob[1], gall[p, t, 1], src[j, p % 4, :, cols])
                dst[j, p % 4, :, cols] = jnp.where(is_glob[0], gall[p, t, 0], value)


def in_hbm(value):
    return pltpu.with_memory_space_constraint(value, pltpu.HBM)


def body(queries, key_vectors, value_vectors, out_grad, rand_blocks, global_blocks):
    vmem = pl.BlockSpec(memory_space=pltpu.VMEM)
    smem = pl.BlockSpec(memory_space=pltpu.SMEM)
    hbm = pl.BlockSpec(memory_space=pl.ANY)
    off = pl.BlockSpec(memory_space=pltpu.HBM)
    shape = jax.ShapeDtypeStruct
    dma = pltpu.SemaphoreType.DMA
    rows = (2, 4, 16, HEADS * HD)
    rand = rand_blocks.T
    yz, zy = ("y", "z"), ("z", "y")
    ga, gb = GATHER_SEMS[yz], GATHER_SEMS[zy]
    mk, mv = REDUCE_MSGS[zy], REDUCE_MSGS[yz]
    att, dq, contrib, dense, near_sum, gout, rand_sib = pl.pallas_call(
        kernel_a,
        name="exchange_and_attend",
        out_shape=(
            shape(rows, BF16),
            shape(rows, BF16),
            shape((8, SLOTS + 2, 2, BLOCK, HD), BF16),
            shape((PLANE, 2, HD, HD), F32),
            shape((2, HD, HD), F32),
            shape((2, 2, 16, HD), BF16),
            shape((3, 16), jnp.int32),
        ),
        in_specs=[off] * 6,
        out_specs=(vmem, vmem, vmem, vmem, vmem, vmem, hbm),
        scratch_shapes=[
            pltpu.VMEM((2, PLANE, 2, BLOCK, HD), BF16),
            pltpu.VMEM((2, PLANE, 2, BLOCK, HD), BF16),
            pltpu.VMEM((PLANE, 64, HD), BF16),
            pltpu.VMEM((mv, 64, HD), BF16),
            pltpu.VMEM((mv, 64, HD), BF16),
            pltpu.VMEM((8, 2, 2, 16, HD), BF16),
            *[pltpu.VMEM((2, 4, BLOCK, HD), BF16)] * 4,
            pltpu.VMEM((2, 2, 13, BLOCK, HD), BF16),
            pltpu.VMEM((2, 3, 9, BLOCK, HD), BF16),
            pltpu.VMEM((8, 32, HD), F32),
            pltpu.VMEM((8, 2, 32, HD), F32),
            pltpu.SMEM((3, 16), jnp.int32),
            pltpu.SMEM((2,), jnp.int32),
            pltpu.VMEM(rows, BF16),
            pltpu.VMEM(rows, BF16),
            pltpu.VMEM((32, PLANE * HD), F32),
            pltpu.VMEM((32, PLANE * HD), F32),
            pltpu.VMEM((32, PLANE * HD), BF16),
            pltpu.VMEM((32, PLANE * HD), BF16),
            pltpu.VMEM((32, HD), BF16),
            pltpu.VMEM((32, HD), BF16),
            pltpu.VMEM((512, HD), BF16),
            pltpu.VMEM((512, HD), BF16),
            pltpu.VMEM((1024, HD), BF16),
            pltpu.VMEM((1024, HD), BF16),
            pltpu.VMEM((2, 512, HD), F32),
            pltpu.VMEM((4, HD, HD), F32),
            dma((1,)), dma((ga,)), dma((1,)), dma((gb,)), dma((1,)), dma((mv,)),
            dma((8,)), dma((8,)), dma((12,)), dma((12,)), dma((12,)), dma((12,)), dma((6,)),
        ],
        compiler_params=pltpu.CompilerParams(
            collective_id=0, has_side_effects=True, vmem_limit_bytes=VMEM_A
        ),
    )(
        *[
            in_hbm(value)
            for value in (
                rand, global_blocks, queries.reshape(rows), key_vectors.reshape(2, BLOCK, HD),
                value_vectors.reshape(2, BLOCK, HD), out_grad.reshape(rows),
            )
        ]
    )
    acc = pl.pallas_call(
        kernel_b,
        name="spread_terms",
        out_shape=shape((PLANE, 2, HD, HD), F32),
        in_specs=[off, smem, off, vmem, vmem],
        out_specs=vmem,
        scratch_shapes=[pltpu.SMEM((3, 16), jnp.int32), pltpu.SMEM((2,), jnp.int32), dma((2,))],
        input_output_aliases={4: 0},
        compiler_params=pltpu.CompilerParams(vmem_limit_bytes=VMEM_B),
    )(in_hbm(rand), rand_sib, in_hbm(global_blocks), contrib, dense)
    sums, gall = pl.pallas_call(
        kernel_c,
        name="reduce_and_gather",
        out_shape=(shape((2, HD, HD), F32), shape((PLANE, 2, 2, 16, HD), BF16)),
        in_specs=[vmem] * 2,
        out_specs=(vmem,) * 2,
        scratch_shapes=[
            pltpu.VMEM((mk, HD, HD), BF16), pltpu.VMEM((mk, HD, HD), BF16),
            pltpu.VMEM((mv, HD, HD), BF16), pltpu.VMEM((mv, HD, HD), BF16),
            dma((1,)), dma((mk,)), dma((1,)), dma((mv,)),
            dma((1,)), dma((ga,)), dma((1,)), dma((gb,)), dma((1,)),
        ],
        compiler_params=pltpu.CompilerParams(
            collective_id=1, has_side_effects=True, vmem_limit_bytes=VMEM_C
        ),
    )(acc, gout)
    att, dq, dk, dv = pl.pallas_call(
        kernel_d,
        name="finish",
        out_shape=(shape(rows, BF16), shape(rows, BF16), shape((HD, HD), BF16), shape((HD, HD), BF16)),
        in_specs=[off] + [vmem] * 5,
        out_specs=(vmem,) * 4,
        scratch_shapes=[pltpu.SMEM((2,), jnp.int32), dma((1,))],
        compiler_params=pltpu.CompilerParams(vmem_limit_bytes=VMEM_D),
    )(in_hbm(global_blocks), sums, near_sum, att, dq, gall)
    return att.reshape(queries.shape), dq.reshape(queries.shape), dk, dv


def solution(mesh):
    assert (mesh.shape["pb"], mesh.shape["ka"]) == (32, 8)
    rows = P(("pb", "ka"), None)
    return jax.shard_map(
        body,
        mesh=mesh,
        in_specs=(rows, rows, rows, rows, P("pb", None), P()),
        out_specs=(rows, rows, rows, rows),
        check_vma=False,
    )
```

```python
import math

import jax
import jax.numpy as jnp
from jax import lax
from jax.experimental import pallas as pl
from jax.experimental.pallas import tpu as pltpu
from jax.sharding import PartitionSpec as P

NX, NY, NZ = 4, 4, 8
PLANE = NY * NZ
SHARDS = 256
NBLK = 512
BLOCK = 64
HD = 128
HEADS = 8
SLOTS = 8
SCALE = 1.0 / math.sqrt(HD)
NEG = -1e30
VMEM_A, VMEM_B, VMEM_C, VMEM_D = 28 << 20, 14 << 20, 14 << 20, 8 << 20
MESH = pl.DeviceIdType.MESH
F32, BF16 = jnp.float32, jnp.bfloat16


def here():
    pb, ka = lax.axis_index("pb"), lax.axis_index("ka")
    return ka % 4, pb // 8, (ka // 4) * 4 + (pb // 2) % 4, pb % 2


def device(x, y, z, c):
    return ((y * 4 + z % 4) * 2 + c, (z // 4) * 4 + x)


def place(block):
    shard = block // 2
    pb, ka = shard // 8, shard % 8
    return ka % 4, pb % 2, (pb // 8) * 8 + (ka // 4) * 4 + (pb // 2) % 4, block % 2


def remote(src, dst, ssem, rsem, dev):
    return pltpu.make_async_remote_copy(
        src_ref=src, dst_ref=dst, send_sem=ssem, recv_sem=rsem, device_id=dev, device_id_type=MESH
    )


RATE, CORE_RATE, LATENCY, AHEAD, FAVOUR = 70.0, 200.0, 1.6, 2.0, 0


def schedule(msgs, favoured=()):
    depth, changed = [1] * len(msgs), True
    while changed:
        changed = False
        for i in range(len(msgs) - 1, -1, -1):
            for dep in msgs[i][0]:
                if depth[dep] <= depth[i]:
                    depth[dep], changed = depth[i] + 1, True
    ranked = sorted(range(len(msgs)), key=lambda i: (-depth[i] - (FAVOUR if i in favoured else 0), i))
    now, free, arrival, come, order = 0.0, {}, {}, set(), []
    while len(come) < len(msgs):
        for i in ranked:
            deps, link, size, work = msgs[i][:4]
            begin = now if link is None else max(free.get(link, 0.0), now)
            if i in arrival or begin > now + AHEAD or any(dep not in come for dep in deps):
                continue
            now += work
            if link is None:
                arrival[i] = now + size
            else:
                free[link] = max(begin, now) + size / (CORE_RATE if link == "core" else RATE)
                arrival[i] = free[link] + LATENCY
            order.append(("send", i))
        i = min((i for i in arrival if i not in come), key=lambda i: (arrival[i], i))
        now = max(now, arrival[i]) + 0.05
        come.add(i)
        order.append(("wait", i))
    return order


def play(flows, more=None, after=None, favour=None):
    msgs, members = [], []
    for own, end in flows:
        base = len(msgs)
        members.append(list(range(base, base + len(own))))
        msgs += [([dep + base for dep in m[0]],) + m[1:] for m in own]
    first = len(msgs)
    if after is not None:
        msgs = [(m[0] or after(first),) + m[1:] for m in msgs]
    if more is not None:
        msgs += more(members)
    for what, i in schedule(msgs, () if favour is None else members[favour]):
        msgs[i][4 if what == "send" else 5]()
    for own, end in flows:
        end()


def ring_around(order, pos, core):
    x, y, z = pos

    def at(o1, o2):
        oy, oz = (o1, o2) if order[0] == "y" else (o2, o1)
        return (y + oy + NY) % NY, (z + oz + NZ) % NZ

    def dev(axis, d):
        step = 1 if d == 0 else -1
        if axis == "y":
            return device(x, (y + step + NY) % NY, z, core)
        return device(x, y, (z + step + NZ) % NZ, core)

    return at, dev, RING[order[0]], RING[order[1]]


RING = {"y": NY, "z": NZ}


def gather_flow(piece, half, order, pos, core, sems, arrived, kb, whole):
    ssem, rsem = sems
    at, dev, n1, n2 = ring_around(order, pos, core)
    msgs, index, seen = [], {}, {}

    def message(deps, o1, o2, nxt, d, halved, axis):
        i = len(msgs)

        def copy(a, b):
            cy, cz = at(a, b)
            ref = half(cy, cz, d) if halved else piece(cy, cz)
            return remote(ref, ref, ssem.at[0], rsem.at[i], dev(axis, d))

        def send():
            copy(o1, o2).start()

        def wait():
            copy(*nxt).wait_recv()
            spot = tuple(abs(o) if abs(o) == n // 2 else o for o, n in zip(nxt, (n1, n2)))
            seen[spot] = seen.get(spot, 0) + 1
            if seen[spot] == (2 if halved else 1):
                arrived(*at(*nxt))

        msgs.append((deps, (axis, d), kb / 2 if halved else kb, 0.02, send, wait))
        return i

    for k in range(n1 // 2):
        for d in (0, 1):
            sign = -1 if d == 0 else 1
            deps = [index[1, sign * k, d]] if k else []
            i = message(deps, sign * k, 0, (sign * (k + 1), 0), d, k == n1 // 2 - 1, order[0])
            index[1, sign * (k + 1), d] = i
    offsets = [0] + [s * k for k in range(1, n1 // 2) for s in (-1, 1)] + [n1 // 2]
    for o in offsets:
        if o == 0:
            first = []
        elif o == n1 // 2:
            first = [index[1, -o, 0], index[1, o, 1]]
        else:
            first = [index[1, o, 0 if o < 0 else 1]]
        for k in range(n2 // 2):
            for d in (0, 1):
                sign = -1 if d == 0 else 1
                deps = [index[2, o, sign * k, d]] if k else first
                i = message(deps, o, sign * k, (o, sign * (k + 1)), d, k == n2 // 2 - 1, order[1])
                index[2, o, sign * (k + 1), d] = i

    def end():
        remote(whole, whole, ssem.at[0], rsem.at[0], dev("y", 0)).wait_send()

    return msgs, end


GATHER_SEMS = {("y", "z"): NY + NY * NZ, ("z", "y"): NZ + NZ * NY}


def reduce_flow(own, got, out, order, pos, core, sems, done, kb):
    ssem, rsem = sems
    at, dev, n1, n2 = ring_around(order, pos, core)
    rows = got.shape[1] // 2
    msgs = []

    def half_of(ref, d):
        return ref.at[pl.ds(d * rows, rows)]

    def load(ref, h):
        return (ref[...] if h is None else half_of(ref, h)[...]).astype(F32)

    def ring(n, axis, term, deps_of):
        steps = n // 2
        base = len(msgs)
        for d in (0, 1):
            for t in range(steps):
                o = (1 if d == 0 else -1) * (steps - t)
                i = base + d * steps + t
                deps = list(deps_of(o)) + ([i - 1] if t else [])

                def copy(i=i, t=t, d=d):
                    src, dst = out.at[i], got.at[i]
                    if t == 0:
                        src, dst = half_of(src, d), half_of(dst, d)
                    return remote(src, dst, ssem.at[0], rsem.at[i], dev(axis, d))

                def send(i=i, o=o, t=t, d=d, copy=copy):
                    value = term(o)
                    if t == 0:
                        half_of(out.at[i], d)[...] = value(d).astype(BF16)
                    elif t == 1:
                        half_of(out.at[i], d)[...] = (value(d) + load(got.at[i - 1], d)).astype(BF16)
                        half_of(out.at[i], 1 - d)[...] = value(1 - d).astype(BF16)
                    else:
                        out[i] = (value(None) + load(got.at[i - 1], None)).astype(BF16)
                    copy().start()

                def wait(copy=copy):
                    copy().wait_recv()

                msgs.append((deps, (axis, d), kb if t else kb / 2, 0.005 * kb, send, wait))
        return base

    offsets = [n2 // 2] + [s * k for k in range(n2 // 2 - 1, 0, -1) for s in (-1, 1)] + [0]
    ends = {}
    for o2 in offsets:

        def term(o1, o2=o2):
            ref = own(*at(o1, o2))
            return lambda h: load(ref, h)

        base = ring(n1, order[0], term, lambda o: [])
        ends[o2] = (base + n1 // 2 - 1, base + n1 - 1)
    ends[-(n2 // 2)] = ends[n2 // 2]

    def term2(o2):
        a, b = ends[o2]
        ref = own(*at(0, o2))
        return lambda h: load(ref, h) + load(got.at[a], h) + load(got.at[b], h)

    base = ring(n2, order[1], term2, lambda o: ends[o])

    def result():
        last = (base + n2 // 2 - 1, base + n2 - 1)
        return term2(0)(None) + load(got.at[last[0]], None) + load(got.at[last[1]], None)

    def end():
        if done is not None:
            done(result())
        whole = out.at[pl.ds(0, PLANE - 1)]
        remote(whole, whole, ssem.at[0], rsem.at[0], dev("y", 0)).wait_send()

    return (msgs, end), result


REDUCE_MSGS = {("y", "z"): NY * NZ + NZ, ("z", "y"): NZ * NY + NY}


def greet(devices):
    barrier = pltpu.get_barrier_semaphore()
    for dev in devices:
        pl.semaphore_signal(barrier, inc=1, device_id=dev, device_id_type=MESH)
    pl.semaphore_wait(barrier, len(devices))


def nt(a, b):
    return lax.dot_general(a, b, (((1,), (1,)), ((), ())), preferred_element_type=F32)


def tn(a, b):
    return lax.dot_general(a, b, (((0,), (0,)), ((), ())), preferred_element_type=F32)


def nn(a, b):
    return lax.dot_general(a, b, (((1,), (0,)), ((), ())), preferred_element_type=F32)


def kernel_a(
    rand_any, glob_any, q_any, k, v, d_any,
    att, dq, contrib, dense, near_sum, gout, rand_sib,
    col_k, col_v, gown, g_got, g_out_buf, sel, xm_a, xm_b, xm_c, xm_d, xs, xall, stat, part,
    rand, glob, q, d, sg, dpg, gp, gs, gq, gd, kc, vc, qs, ds_, dkv, own_sum,
    a_ssem, a_rsem, b_ssem, b_rsem, g_ssem, g_rsem, c_ssem, c_rsem, x_ssem, x_rsem, ssem, rsem, lsem,
):
    x, y, z, c = here()
    col, xm = (col_k, col_v), ((xm_a, xm_b), (xm_c, xm_d))
    pb, ka = lax.axis_index("pb"), lax.axis_index("ka")
    shard = pb * 8 + ka
    me = y * NZ + z
    row = c * 4 + x
    zh = z // 4
    pos = (x, y, z)

    def row_dev(r):
        return device(r % 4, y, z, r // 4)

    def x_dev(step):
        return device((x + step + 4) % 4, y, z, c)

    row_peers = [(row + i) % 8 for i in range(1, 8)]
    sibling = row_dev((row + 4) % 8)

    local = [
        pltpu.make_async_copy(k, col[0].at[c, me], lsem.at[0]),
        pltpu.make_async_copy(v, col[1].at[c, me], lsem.at[1]),
        pltpu.make_async_copy(q_any, q, lsem.at[2]),
        pltpu.make_async_copy(d_any, d, lsem.at[3]),
        pltpu.make_async_copy(rand_any, rand, lsem.at[4]),
        pltpu.make_async_copy(glob_any, glob, lsem.at[5]),
    ]
    for cp in local:
        cp.start()
    greet(
        [
            device(x, (y + 1) % NY, z, c), device(x, (y + NY - 1) % NY, z, c),
            device(x, y, (z + 1) % NZ, c), device(x, y, (z + NZ - 1) % NZ, c),
        ]
        + [row_dev(r) for r in row_peers]
    )
    for cp in local:
        cp.wait()
    rand_copy = remote(rand_any, rand_sib, ssem.at[2], rsem.at[2], sibling)
    rand_copy.start()

    def pass_on(kv):
        def arrived(py, pz):
            ref = col[kv].at[c, py * NZ + pz]
            remote(ref, ref, ssem.at[3 + kv], rsem.at[3 + kv], sibling).start()

        return arrived

    def piece(kv):
        return lambda py, pz: col[kv].at[c, py * NZ + pz]

    def half(kv):
        return lambda py, pz, h: col[kv].at[c, py * NZ + pz, h]

    def some(kv):
        return col[kv].at[0, pl.ds(0, PLANE - 1)]

    flow_k = gather_flow(
        piece(0), half(0), ("y", "z"), pos, c, (a_ssem, a_rsem), pass_on(0), 32, some(0)
    )
    flow_v = gather_flow(
        piece(1), half(1), ("z", "y"), pos, c, (b_ssem, b_rsem), pass_on(1), 32, some(1)
    )
    pass_on(0)(y, z)
    pass_on(1)(y, z)

    g_place = [place(glob[g]) for g in range(2)]
    shards = jnp.full((16, HD), shard, jnp.int32)
    for g in range(2):
        mine = shards == glob[g] // 2
        for t, ref in ((0, q), (1, d)):
            for p in range(PLANE):
                value = ref[g_place[g][3], p % 4, :, (p // 4) * HD : (p // 4 + 1) * HD]
                rows = slice((g * 2 + t) * 16, (g * 2 + t + 1) * 16)
                gown[p, rows, :] = jnp.where(mine, value, jnp.zeros_like(value))

    flow_g, tiles = reduce_flow(
        lambda py, pz: gown.at[py * NZ + pz], g_got, g_out_buf, ("y", "z"), pos, c, (g_ssem, g_rsem),
        None, 16,
    )

    for j in range(2):
        for h in range(HEADS):
            rows = pl.ds(j * 512 + h * 64, 64)
            qs[rows, :] = q[j, :, :, h * HD : (h + 1) * HD].reshape(64, HD)
            ds_[rows, :] = d[j, :, :, h * HD : (h + 1) * HD].reshape(64, HD)

    def send_sel():
        sel[row] = tiles().reshape(2, 2, 16, HD).astype(BF16)
        for r in row_peers:
            remote(sel.at[row], sel.at[row], ssem.at[6], rsem.at[6], row_dev(r)).start()

    def wait_sel():
        remote(sel.at[pl.ds(0, 7)], sel.at[pl.ds(0, 7)], ssem.at[6], rsem.at[6], sibling).wait_recv()

    def wanted(ka_of, slot):
        if slot >= 6:
            return glob[slot - 6]
        return rand[slot % 3, ka_of * 2 + slot // 3]

    def ka_at(step):
        return zh * 4 + (x + step + 4) % 4

    def slot_at(direction, i):
        return i if direction == 0 else (i + 4) % 8

    def block_of(kv, block):
        bx, bc, bp, bh = place(block)
        return col[kv][bc, bp, bh]

    def x_copy(kv, dr, kind):
        src, dst = (
            (xs.at[kv, dr, pl.ds(9, 4)], xm[kv][dr].at[0]),
            (xs.at[kv, dr, pl.ds(4, 5)], xall.at[kv, dr, pl.ds(4, 5)]),
            (xs.at[kv, dr, pl.ds(0, 4)], xall.at[kv, dr, pl.ds(0, 4)]),
        )[kind]
        sem = kv * 6 + dr * 3 + kind
        return remote(src, dst, x_ssem.at[sem], x_rsem.at[sem], x_dev(1 - 2 * dr))

    def column_in(kv):
        ref = col[kv].at[1 - c]
        remote(ref, ref, ssem.at[3 + kv], rsem.at[3 + kv], sibling).wait_recv()

    def send_far(kv, dr):
        for i in range(4):
            xs[kv, dr, 9 + i] = block_of(kv, wanted(ka_at(2), slot_at(dr, i)))
        x_copy(kv, dr, 0).start()

    def send_near(kv, dr):
        step = 1 - 2 * dr
        for i in range(4, 8):
            xs[kv, dr, i] = block_of(kv, wanted(ka_at(step), slot_at(dr, i)))
        to = pb * 8 + ka_at(step)
        edge = (to * 2 + 2 * SHARDS - 1) % NBLK if dr == 0 else (to * 2 + 2) % NBLK
        xs[kv, dr, 8] = block_of(kv, edge)
        x_copy(kv, dr, 1).start()
        for i in range(4):
            xm[kv][dr][1, i] = block_of(kv, wanted(ka_at(step), slot_at(dr, i)))
        for i in range(4):
            xall[kv, 2, dr * 4 + i] = block_of(kv, wanted(ka, dr * 4 + i))

    def send_merged(kv, dr):
        for i in range(4):
            bx = place(wanted(ka_at(1 - 2 * dr), slot_at(dr, i)))[0]
            xs[kv, dr, i] = xm[kv][dr][jnp.where(bx == x, 1, 0), i]
        x_copy(kv, dr, 2).start()

    def global_scores():
        for g in range(2):
            gx, gc, gpl, gh = g_place[g]
            gq[pl.ds(g * 16, 16), :] = sel[gc * 4 + gx, g, 0]
            gd[pl.ds(g * 16, 16), :] = sel[gc * 4 + gx, g, 1]
        for i in range(4):
            lanes, ps = slice(i * 1024, (i + 1) * 1024), pl.ds(i * 8, 8)
            sg[:, lanes] = nt(gq[...], col[0][c, ps].reshape(1024, HD)) * SCALE
            dpg[:, lanes] = nt(gd[...], col[1][c, ps].reshape(1024, HD))
        g_max = jnp.max(sg[...], axis=1, keepdims=True)
        g_exp = jnp.exp(sg[...] - g_max)
        g_sum = jnp.sum(g_exp, axis=1, keepdims=True)
        g_dot = jnp.sum(g_exp * dpg[...], axis=1, keepdims=True)
        lane = lax.broadcasted_iota(jnp.int32, (32, HD), 1)
        stat[row] = jnp.where(lane == 0, g_max, jnp.where(lane == 1, g_sum, g_dot))
        for r in row_peers:
            remote(stat.at[row], stat.at[row], ssem.at[8], rsem.at[8], row_dev(r)).start()

    nothing = lambda: None

    def exchange(members):
        keys, values, rows_g = members
        n = len(keys) + len(values) + len(rows_g)
        more = [(rows_g, None, 2.5, 0.1, send_sel, wait_sel)]
        for kv, flow in ((0, keys), (1, values)):
            here_in = n + len(more)
            more.append((flow, None, 1.6, 0.0, nothing, lambda kv=kv: column_in(kv)))
            far = n + len(more)
            for kind, send, deps, kb in (
                (0, send_far, lambda dr: [here_in], 64),
                (1, send_near, lambda dr: [here_in], 80),
                (2, send_merged, lambda dr: [here_in, far + dr, far + 2 + dr], 64),
            ):
                for dr in range(2):
                    more.append(
                        (
                            deps(dr), ("x", dr), kb, 0.2,
                            lambda kv=kv, dr=dr, send=send: send(kv, dr),
                            lambda kv=kv, dr=dr, kind=kind: x_copy(kv, dr, kind).wait_recv(),
                        )
                    )
        more.append((keys + values + [n], None, 0.1, 1.5, global_scores, nothing))
        return more

    play((flow_k, flow_v, flow_g), exchange, favour=0)

    slot_of = lax.broadcasted_iota(jnp.int32, (1, 512), 1) // BLOCK
    for j in range(2):
        block = shard * 2 + j
        cand = [block - 1, block, block + 1, glob[0], glob[1]]
        cand += [rand[r, ka * 2 + j] for r in range(3)]
        for kv, dst in ((0, kc), (1, vc)):
            near_refs = [xall.at[kv, 0, 8], col[kv].at[c, me, 0], col[kv].at[c, me, 1], xall.at[kv, 1, 8]]
            for i in range(3):
                dst[i * BLOCK : (i + 1) * BLOCK, :] = near_refs[i + j][...]
            for i in range(3, 8):
                slot = 6 + i - 3 if i < 5 else j * 3 + i - 5
                far = 0 if slot < 4 else 1
                off = (place(cand[i])[0] + 4 - x) % 4
                src = jnp.where(off == 0, 2, jnp.where(off == 3, 0, jnp.where(off == 1, 1, far)))
                spot = jnp.where(src == 1, (slot + 4) % 8, slot)
                dst[i * BLOCK : (i + 1) * BLOCK, :] = xall[kv, src, spot]
        cands = jnp.zeros((1, 512), jnp.int32)
        for i in range(8):
            cands = jnp.where(slot_of == i, cand[i], cands)
        out = (cands < 0) | (cands >= NBLK)
        for i in range(7):
            out = out | ((slot_of > i) & (cands == cand[i]))
        bias = jnp.where(out, NEG, 0.0)
        blocks = jnp.full((256, 1), block, jnp.int32)
        keep = jnp.where((blocks == glob[0]) | (blocks == glob[1]), 0.0, 1.0)
        for part_i in range(2):
            rows = pl.ds(j * 512 + part_i * 256, 256)
            qv, dv = qs[rows, :], ds_[rows, :]
            s = nt(qv, kc[...]) * SCALE + bias
            e = jnp.exp(s - jnp.max(s, axis=1, keepdims=True))
            w = e * (keep / jnp.sum(e, axis=1, keepdims=True))
            wb = w.astype(BF16)
            o = nn(wb, vc[...]).astype(BF16)
            dot = jnp.sum(dv.astype(F32) * o.astype(F32), axis=1, keepdims=True)
            ds = (w * (nt(dv, vc[...]) - dot)).astype(BF16)
            dqv = (nn(ds, kc[...]) * SCALE).astype(BF16)
            for h in range(4):
                cols = slice((part_i * 4 + h) * HD, (part_i * 4 + h + 1) * HD)
                att[j, :, :, cols] = o[h * 64 : (h + 1) * 64].reshape(4, 16, HD)
                dq[j, :, :, cols] = dqv[h * 64 : (h + 1) * 64].reshape(4, 16, HD)
            dk_new, dv_new = tn(ds, qv) * SCALE, tn(wb, dv)
            if part_i == 0:
                dkv[0], dkv[1] = dk_new, dv_new
            else:
                dkv[0] += dk_new
                dkv[1] += dv_new
        for kv in range(2):
            for i in range(8):
                term = dkv[kv, i * BLOCK : (i + 1) * BLOCK, :]
                spot = i + j - 1
                if i < 3 and spot in (-1, 2):
                    contrib[row, 9 if spot == -1 else 0, kv] = term.astype(BF16)
                elif i < 3:
                    if (j, i) in ((0, 1), (0, 2)):
                        own_sum[kv, pl.ds(spot * BLOCK, BLOCK), :] = term
                    else:
                        total = own_sum[kv, pl.ds(spot * BLOCK, BLOCK), :] + term
                        near_sum[kv, pl.ds(spot * BLOCK, BLOCK), :] = total
                elif i >= 5:
                    contrib[row, 1 + j * 3 + i - 5, kv] = term.astype(BF16)
                elif j == 0:
                    own_sum[2 + kv, pl.ds((i - 3) * BLOCK, BLOCK), :] = term
                else:
                    total = own_sum[2 + kv, pl.ds((i - 3) * BLOCK, BLOCK), :] + term
                    contrib[row, 7 + i - 3, kv] = total.astype(BF16)

    def c_copy(src, first, n, step, sem):
        ref = contrib.at[src, pl.ds(first, n)]
        dev = sibling if step is None else x_dev(step)
        return remote(ref, ref, c_ssem.at[sem], c_rsem.at[sem], dev)

    def at_x(o):
        return c * 4 + (x + o + 4) % 4

    c_sends = [c_copy(row, 0, 9, 1, 0), c_copy(row, 1, 9, -1, 1), c_copy(row, 1, 8, None, 4)]
    for cp in c_sends:
        cp.start()

    remote(stat.at[pl.ds(0, 7)], stat.at[pl.ds(0, 7)], ssem.at[8], rsem.at[8], sibling).wait_recv()
    stats = [stat[i] for i in range(8)]
    top = stats[0][:, 0:1]
    for i in range(1, 8):
        top = jnp.maximum(top, stats[i][:, 0:1])
    total, dot = jnp.zeros((32, 1), F32), jnp.zeros((32, 1), F32)
    for i in range(8):
        f = jnp.exp(stats[i][:, 0:1] - top)
        total += stats[i][:, 1:2] * f
        dot += stats[i][:, 2:3] * f
    g_row = lax.broadcasted_iota(jnp.int32, (32, 1), 0)
    g_one = jnp.full((32, 1), glob[1], jnp.int32)
    first = jnp.where((g_row >= 16) & (g_one == glob[0]), 0.0, 1.0)
    gw = jnp.exp(sg[...] - top) * (first / total)
    gp[...] = gw.astype(BF16)
    gs[...] = (gw * (dpg[...] - dot / total)).astype(BF16)
    g_o, g_dq = jnp.zeros((32, HD), F32), jnp.zeros((32, HD), F32)
    for i in range(4):
        lanes, ps = slice(i * 1024, (i + 1) * 1024), pl.ds(i * 8, 8)
        g_o += nn(gp[:, lanes], col[1][c, ps].reshape(1024, HD))
        g_dq += nn(gs[:, lanes], col[0][c, ps].reshape(1024, HD))
    part[row, 0] = g_o
    part[row, 1] = g_dq * SCALE
    for r in row_peers:
        remote(part.at[row], part.at[row], ssem.at[11], rsem.at[11], row_dev(r)).start()

    c_copy(at_x(-1), 0, 9, 1, 0).wait_recv()
    more = [c_copy(at_x(-1), 1, 4, 1, 2), c_copy(at_x(-1), 0, 9, None, 5)]
    for cp in more:
        cp.start()
    c_copy(at_x(1), 1, 9, -1, 1).wait_recv()
    more += [c_copy(at_x(1), 5, 4, -1, 3), c_copy(at_x(1), 1, 9, None, 6)]
    for cp in more[2:]:
        cp.start()
    c_sends += more

    for i in range(4):
        lanes, ps = slice(i * 1024, (i + 1) * 1024), pl.ds(i * 8, 8)
        dense[ps, 0] = (tn(gs[:, lanes], gq[...]) * SCALE).reshape(8, HD, HD)
        dense[ps, 1] = tn(gp[:, lanes], gd[...]).reshape(8, HD, HD)

    c_copy(at_x(2), 1, 4, 1, 2).wait_recv()
    c_copy(at_x(2), 5, 4, -1, 3).wait_recv()
    last = c_copy(at_x(2), 1, 8, None, 7)
    last.start()
    c_sends.append(last)

    remote(part.at[pl.ds(0, 7)], part.at[pl.ds(0, 7)], ssem.at[11], rsem.at[11], sibling).wait_recv()
    for t in range(2):
        acc = part[0, t]
        for i in range(1, 8):
            acc += part[i, t]
        for g in range(2):
            gout[t, g] = acc[g * 16 : (g + 1) * 16].astype(BF16)

    def at_other(o):
        return (1 - c) * 4 + (x + o + 4) % 4

    for sem, o, first, n in ((4, 0, 1, 8), (5, -1, 0, 9), (6, 1, 1, 9), (7, 2, 1, 8)):
        c_copy(at_other(o), first, n, None, sem).wait_recv()
    rand_copy.wait_recv()

    for cp in c_sends + [rand_copy]:
        cp.wait_send()
    for kv in range(2):
        remote(col[kv].at[c], col[kv].at[c], ssem.at[3 + kv], rsem.at[3 + kv], sibling).wait_send()
    for ref, sem in ((sel, 6), (stat, 8), (part, 11)):
        remote(ref.at[pl.ds(0, 7)], ref.at[pl.ds(0, 7)], ssem.at[sem], rsem.at[sem], sibling).wait_send()
    for kv in range(2):
        for dr in range(2):
            for kind in range(3):
                x_copy(kv, dr, kind).wait_send()


def kernel_b(rand_any, rand_sib, glob_any, contrib, dense, acc, rand, glob, sem):
    x, y, z, c = here()
    zh = z // 4
    del dense
    copies = [
        pltpu.make_async_copy(rand_any, rand, sem.at[0]),
        pltpu.make_async_copy(glob_any, glob, sem.at[1]),
    ]
    for cp in copies:
        cp.start()
    for cp in copies:
        cp.wait()

    def add(block, here_too, src, entry):
        bx, bc, bp, bh = place(block)

        @pl.when(here_too & (bx == x) & (bc == c))
        def _():
            rows = pl.ds(pl.multiple_of(bh * BLOCK, BLOCK), BLOCK)
            acc[bp, :, rows, :] += contrib[src, entry].astype(F32)

    for core in range(2):
        for xs in range(NX):
            src = core * 4 + xs
            shard = ((y * 4 + z % 4) * 2 + core) * 8 + zh * 4 + xs
            for slot in range(SLOTS):
                if slot >= 6:
                    block = glob[slot - 6]
                else:
                    r, s = (zh * 4 + xs) * 2 + slot // 3, slot % 3
                    block = jnp.where(c == core, rand[s, r], rand_sib[s, r])
                add(block, True, src, 1 + slot)
            after, before = shard * 2 + 2, shard * 2 - 1
            add(jnp.minimum(after, NBLK - 1), (after < NBLK) & ((xs - x + 4) % 4 == 3), src, 0)
            add(jnp.maximum(before, 0), (before >= 0) & ((xs - x + 4) % 4 == 1), src, 9)


def kernel_c(
    acc, gout,
    sums, gall,
    got_k, out_k, got_v, out_v,
    k_ssem, k_rsem, v_ssem, v_rsem, o_ssem, o_rsem, w_ssem, w_rsem, lsem,
):
    x, y, z, c = here()
    me = y * NZ + z
    own = pltpu.make_async_copy(gout, gall.at[me], lsem.at[0])
    own.start()
    greet(
        [
            device(x, (y + 1) % NY, z, c), device(x, (y + NY - 1) % NY, z, c),
            device(x, y, (z + 1) % NZ, c), device(x, y, (z + NZ - 1) % NZ, c),
        ]
    )
    own.wait()
    pos = (x, y, z)

    def finish(kv):
        def done(value):
            sums[kv] = value

        return done

    def term(kv):
        return lambda py, pz: acc.at[py * NZ + pz, kv]

    def piece(t):
        return lambda py, pz: gall.at[py * NZ + pz, t]

    def half(t):
        return lambda py, pz, h: gall.at[py * NZ + pz, t, h]

    nothing = lambda py, pz: None
    some = [gall.at[pl.ds(0, PLANE - 1), t] for t in range(2)]
    play(
        (
            reduce_flow(term(0), got_k, out_k, ("z", "y"), pos, c, (k_ssem, k_rsem), finish(0), 32)[0],
            reduce_flow(term(1), got_v, out_v, ("y", "z"), pos, c, (v_ssem, v_rsem), finish(1), 32)[0],
            gather_flow(piece(0), half(0), ("y", "z"), pos, c, (o_ssem, o_rsem), nothing, 8, some[0]),
            gather_flow(piece(1), half(1), ("z", "y"), pos, c, (w_ssem, w_rsem), nothing, 8, some[1]),
        )
    )


def kernel_d(glob_any, sums, near_sum, att_in, dq_in, gall, att, dq, dk, dv, glob, sem):
    cp = pltpu.make_async_copy(glob_any, glob, sem.at[0])
    cp.start()
    shard = lax.axis_index("pb") * 8 + lax.axis_index("ka")
    dk[...] = (sums[0] + near_sum[0]).astype(BF16)
    dv[...] = (sums[1] + near_sum[1]).astype(BF16)
    cp.wait()
    for j in range(2):
        blocks = jnp.full((16, HD), shard * 2 + j, jnp.int32)
        is_glob = [blocks == glob[g] for g in range(2)]
        for t, src, dst in ((0, att_in, att), (1, dq_in, dq)):
            for p in range(PLANE):
                cols = slice((p // 4) * HD, (p // 4 + 1) * HD)
                value = jnp.where(is_glob[1], gall[p, t, 1], src[j, p % 4, :, cols])
                dst[j, p % 4, :, cols] = jnp.where(is_glob[0], gall[p, t, 0], value)


def in_hbm(value):
    return pltpu.with_memory_space_constraint(value, pltpu.HBM)


def body(queries, key_vectors, value_vectors, out_grad, rand_blocks, global_blocks):
    vmem = pl.BlockSpec(memory_space=pltpu.VMEM)
    smem = pl.BlockSpec(memory_space=pltpu.SMEM)
    hbm = pl.BlockSpec(memory_space=pl.ANY)
    off = pl.BlockSpec(memory_space=pltpu.HBM)
    shape = jax.ShapeDtypeStruct
    dma = pltpu.SemaphoreType.DMA
    rows = (2, 4, 16, HEADS * HD)
    rand = rand_blocks.T
    yz, zy = ("y", "z"), ("z", "y")
    ga, gb = GATHER_SEMS[yz], GATHER_SEMS[zy]
    mk, mv = REDUCE_MSGS[zy], REDUCE_MSGS[yz]
    att, dq, contrib, dense, near_sum, gout, rand_sib = pl.pallas_call(
        kernel_a,
        name="exchange_and_attend",
        out_shape=(
            shape(rows, BF16),
            shape(rows, BF16),
            shape((8, SLOTS + 2, 2, BLOCK, HD), BF16),
            shape((PLANE, 2, HD, HD), F32),
            shape((2, HD, HD), F32),
            shape((2, 2, 16, HD), BF16),
            shape((3, 16), jnp.int32),
        ),
        in_specs=[off] * 6,
        out_specs=(vmem, vmem, vmem, vmem, vmem, vmem, hbm),
        scratch_shapes=[
            pltpu.VMEM((2, PLANE, 2, BLOCK, HD), BF16),
            pltpu.VMEM((2, PLANE, 2, BLOCK, HD), BF16),
            pltpu.VMEM((PLANE, 64, HD), BF16),
            pltpu.VMEM((mv, 64, HD), BF16),
            pltpu.VMEM((mv, 64, HD), BF16),
            pltpu.VMEM((8, 2, 2, 16, HD), BF16),
            *[pltpu.VMEM((2, 4, BLOCK, HD), BF16)] * 4,
            pltpu.VMEM((2, 2, 13, BLOCK, HD), BF16),
            pltpu.VMEM((2, 3, 9, BLOCK, HD), BF16),
            pltpu.VMEM((8, 32, HD), F32),
            pltpu.VMEM((8, 2, 32, HD), F32),
            pltpu.SMEM((3, 16), jnp.int32),
            pltpu.SMEM((2,), jnp.int32),
            pltpu.VMEM(rows, BF16),
            pltpu.VMEM(rows, BF16),
            pltpu.VMEM((32, PLANE * HD), F32),
            pltpu.VMEM((32, PLANE * HD), F32),
            pltpu.VMEM((32, PLANE * HD), BF16),
            pltpu.VMEM((32, PLANE * HD), BF16),
            pltpu.VMEM((32, HD), BF16),
            pltpu.VMEM((32, HD), BF16),
            pltpu.VMEM((512, HD), BF16),
            pltpu.VMEM((512, HD), BF16),
            pltpu.VMEM((1024, HD), BF16),
            pltpu.VMEM((1024, HD), BF16),
            pltpu.VMEM((2, 512, HD), F32),
            pltpu.VMEM((4, HD, HD), F32),
            dma((1,)), dma((ga,)), dma((1,)), dma((gb,)), dma((1,)), dma((mv,)),
            dma((8,)), dma((8,)), dma((12,)), dma((12,)), dma((12,)), dma((12,)), dma((6,)),
        ],
        compiler_params=pltpu.CompilerParams(
            collective_id=0, has_side_effects=True, vmem_limit_bytes=VMEM_A
        ),
    )(
        *[
            in_hbm(value)
            for value in (
                rand, global_blocks, queries.reshape(rows), key_vectors.reshape(2, BLOCK, HD),
                value_vectors.reshape(2, BLOCK, HD), out_grad.reshape(rows),
            )
        ]
    )
    acc = pl.pallas_call(
        kernel_b,
        name="spread_terms",
        out_shape=shape((PLANE, 2, HD, HD), F32),
        in_specs=[off, smem, off, vmem, vmem],
        out_specs=vmem,
        scratch_shapes=[pltpu.SMEM((3, 16), jnp.int32), pltpu.SMEM((2,), jnp.int32), dma((2,))],
        input_output_aliases={4: 0},
        compiler_params=pltpu.CompilerParams(vmem_limit_bytes=VMEM_B),
    )(in_hbm(rand), rand_sib, in_hbm(global_blocks), contrib, dense)
    sums, gall = pl.pallas_call(
        kernel_c,
        name="reduce_and_gather",
        out_shape=(shape((2, HD, HD), F32), shape((PLANE, 2, 2, 16, HD), BF16)),
        in_specs=[vmem] * 2,
        out_specs=(vmem,) * 2,
        scratch_shapes=[
            pltpu.VMEM((mk, HD, HD), BF16), pltpu.VMEM((mk, HD, HD), BF16),
            pltpu.VMEM((mv, HD, HD), BF16), pltpu.VMEM((mv, HD, HD), BF16),
            dma((1,)), dma((mk,)), dma((1,)), dma((mv,)),
            dma((1,)), dma((ga,)), dma((1,)), dma((gb,)), dma((1,)),
        ],
        compiler_params=pltpu.CompilerParams(
            collective_id=1, has_side_effects=True, vmem_limit_bytes=VMEM_C
        ),
    )(acc, gout)
    att, dq, dk, dv = pl.pallas_call(
        kernel_d,
        name="finish",
        out_shape=(shape(rows, BF16), shape(rows, BF16), shape((HD, HD), BF16), shape((HD, HD), BF16)),
        in_specs=[off] + [vmem] * 5,
        out_specs=(vmem,) * 4,
        scratch_shapes=[pltpu.SMEM((2,), jnp.int32), dma((1,))],
        compiler_params=pltpu.CompilerParams(vmem_limit_bytes=VMEM_D),
    )(in_hbm(global_blocks), sums, near_sum, att, dq, gall)
    return att.reshape(queries.shape), dq.reshape(queries.shape), dk, dv


def solution(mesh):
    assert (mesh.shape["pb"], mesh.shape["ka"]) == (32, 8)
    rows = P(("pb", "ka"), None)
    return jax.shard_map(
        body,
        mesh=mesh,
        in_specs=(rows, rows, rows, rows, P("pb", None), P()),
        out_specs=(rows, rows, rows, rows),
        check_vma=False,
    )
```

```python
import math

import jax
import jax.numpy as jnp
from jax import lax
from jax.experimental import pallas as pl
from jax.experimental.pallas import tpu as pltpu
from jax.sharding import PartitionSpec as P

NX, NY, NZ = 4, 4, 8
PLANE = NY * NZ
SHARDS = 256
NBLK = 512
BLOCK = 64
HD = 128
HEADS = 8
SLOTS = 8
SCALE = 1.0 / math.sqrt(HD)
NEG = -1e30
VMEM_A, VMEM_B, VMEM_C, VMEM_D = 28 << 20, 14 << 20, 14 << 20, 8 << 20
MESH = pl.DeviceIdType.MESH
F32, BF16 = jnp.float32, jnp.bfloat16


def here():
    pb, ka = lax.axis_index("pb"), lax.axis_index("ka")
    return ka % 4, pb // 8, (ka // 4) * 4 + (pb // 2) % 4, pb % 2


def device(x, y, z, c):
    return ((y * 4 + z % 4) * 2 + c, (z // 4) * 4 + x)


def place(block):
    shard = block // 2
    pb, ka = shard // 8, shard % 8
    return ka % 4, pb % 2, (pb // 8) * 8 + (ka // 4) * 4 + (pb // 2) % 4, block % 2


def remote(src, dst, ssem, rsem, dev):
    return pltpu.make_async_remote_copy(
        src_ref=src, dst_ref=dst, send_sem=ssem, recv_sem=rsem, device_id=dev, device_id_type=MESH
    )


RATE, CORE_RATE, LATENCY, AHEAD, FAVOUR = 90.0, 200.0, 1.6, 2.0, 0


def schedule(msgs, favoured=()):
    depth, changed = [1] * len(msgs), True
    while changed:
        changed = False
        for i in range(len(msgs) - 1, -1, -1):
            for dep in msgs[i][0]:
                if depth[dep] <= depth[i]:
                    depth[dep], changed = depth[i] + 1, True
    ranked = sorted(range(len(msgs)), key=lambda i: (-depth[i] - (FAVOUR if i in favoured else 0), i))
    now, free, arrival, come, order = 0.0, {}, {}, set(), []
    while len(come) < len(msgs):
        for i in ranked:
            deps, link, size, work = msgs[i][:4]
            begin = now if link is None else max(free.get(link, 0.0), now)
            if i in arrival or begin > now + AHEAD or any(dep not in come for dep in deps):
                continue
            now += work
            if link is None:
                arrival[i] = now + size
            else:
                free[link] = max(begin, now) + size / (CORE_RATE if link == "core" else RATE)
                arrival[i] = free[link] + LATENCY
            order.append(("send", i))
        i = min((i for i in arrival if i not in come), key=lambda i: (arrival[i], i))
        now = max(now, arrival[i]) + 0.05
        come.add(i)
        order.append(("wait", i))
    return order


def play(flows, more=None, after=None, favour=None):
    msgs, members = [], []
    for own, end in flows:
        base = len(msgs)
        members.append(list(range(base, base + len(own))))
        msgs += [([dep + base for dep in m[0]],) + m[1:] for m in own]
    first = len(msgs)
    if after is not None:
        msgs = [(m[0] or after(first),) + m[1:] for m in msgs]
    if more is not None:
        msgs += more(members)
    for what, i in schedule(msgs, () if favour is None else members[favour]):
        msgs[i][4 if what == "send" else 5]()
    for own, end in flows:
        end()


def ring_around(order, pos, core):
    x, y, z = pos

    def at(o1, o2):
        oy, oz = (o1, o2) if order[0] == "y" else (o2, o1)
        return (y + oy + NY) % NY, (z + oz + NZ) % NZ

    def dev(axis, d):
        step = 1 if d == 0 else -1
        if axis == "y":
            return device(x, (y + step + NY) % NY, z, core)
        return device(x, y, (z + step + NZ) % NZ, core)

    return at, dev, RING[order[0]], RING[order[1]]


RING = {"y": NY, "z": NZ}


def gather_flow(piece, half, order, pos, core, sems, arrived, kb, whole):
    ssem, rsem = sems
    at, dev, n1, n2 = ring_around(order, pos, core)
    msgs, index, seen = [], {}, {}

    def message(deps, o1, o2, nxt, d, halved, axis):
        i = len(msgs)

        def copy(a, b):
            cy, cz = at(a, b)
            ref = half(cy, cz, d) if halved else piece(cy, cz)
            return remote(ref, ref, ssem.at[0], rsem.at[i], dev(axis, d))

        def send():
            copy(o1, o2).start()

        def wait():
            copy(*nxt).wait_recv()
            spot = tuple(abs(o) if abs(o) == n // 2 else o for o, n in zip(nxt, (n1, n2)))
            seen[spot] = seen.get(spot, 0) + 1
            if seen[spot] == (2 if halved else 1):
                arrived(*at(*nxt))

        msgs.append((deps, (axis, d), kb / 2 if halved else kb, 0.02, send, wait))
        return i

    for k in range(n1 // 2):
        for d in (0, 1):
            sign = -1 if d == 0 else 1
            deps = [index[1, sign * k, d]] if k else []
            i = message(deps, sign * k, 0, (sign * (k + 1), 0), d, k == n1 // 2 - 1, order[0])
            index[1, sign * (k + 1), d] = i
    offsets = [0] + [s * k for k in range(1, n1 // 2) for s in (-1, 1)] + [n1 // 2]
    for o in offsets:
        if o == 0:
            first = []
        elif o == n1 // 2:
            first = [index[1, -o, 0], index[1, o, 1]]
        else:
            first = [index[1, o, 0 if o < 0 else 1]]
        for k in range(n2 // 2):
            for d in (0, 1):
                sign = -1 if d == 0 else 1
                deps = [index[2, o, sign * k, d]] if k else first
                i = message(deps, o, sign * k, (o, sign * (k + 1)), d, k == n2 // 2 - 1, order[1])
                index[2, o, sign * (k + 1), d] = i

    def end():
        remote(whole, whole, ssem.at[0], rsem.at[0], dev("y", 0)).wait_send()

    return msgs, end


GATHER_SEMS = {("y", "z"): NY + NY * NZ, ("z", "y"): NZ + NZ * NY}


def reduce_flow(own, got, out, order, pos, core, sems, done, kb):
    ssem, rsem = sems
    at, dev, n1, n2 = ring_around(order, pos, core)
    rows = got.shape[1] // 2
    msgs = []

    def half_of(ref, d):
        return ref.at[pl.ds(d * rows, rows)]

    def load(ref, h):
        return (ref[...] if h is None else half_of(ref, h)[...]).astype(F32)

    def ring(n, axis, term, deps_of):
        steps = n // 2
        base = len(msgs)
        for d in (0, 1):
            for t in range(steps):
                o = (1 if d == 0 else -1) * (steps - t)
                i = base + d * steps + t
                deps = list(deps_of(o)) + ([i - 1] if t else [])

                def copy(i=i, t=t, d=d):
                    src, dst = out.at[i], got.at[i]
                    if t == 0:
                        src, dst = half_of(src, d), half_of(dst, d)
                    return remote(src, dst, ssem.at[0], rsem.at[i], dev(axis, d))

                def send(i=i, o=o, t=t, d=d, copy=copy):
                    value = term(o)
                    if t == 0:
                        half_of(out.at[i], d)[...] = value(d).astype(BF16)
                    elif t == 1:
                        half_of(out.at[i], d)[...] = (value(d) + load(got.at[i - 1], d)).astype(BF16)
                        half_of(out.at[i], 1 - d)[...] = value(1 - d).astype(BF16)
                    else:
                        out[i] = (value(None) + load(got.at[i - 1], None)).astype(BF16)
                    copy().start()

                def wait(copy=copy):
                    copy().wait_recv()

                msgs.append((deps, (axis, d), kb if t else kb / 2, 0.005 * kb, send, wait))
        return base

    offsets = [n2 // 2] + [s * k for k in range(n2 // 2 - 1, 0, -1) for s in (-1, 1)] + [0]
    ends = {}
    for o2 in offsets:

        def term(o1, o2=o2):
            ref = own(*at(o1, o2))
            return lambda h: load(ref, h)

        base = ring(n1, order[0], term, lambda o: [])
        ends[o2] = (base + n1 // 2 - 1, base + n1 - 1)
    ends[-(n2 // 2)] = ends[n2 // 2]

    def term2(o2):
        a, b = ends[o2]
        ref = own(*at(0, o2))
        return lambda h: load(ref, h) + load(got.at[a], h) + load(got.at[b], h)

    base = ring(n2, order[1], term2, lambda o: ends[o])

    def result():
        last = (base + n2 // 2 - 1, base + n2 - 1)
        return term2(0)(None) + load(got.at[last[0]], None) + load(got.at[last[1]], None)

    def end():
        if done is not None:
            done(result())
        whole = out.at[pl.ds(0, PLANE - 1)]
        remote(whole, whole, ssem.at[0], rsem.at[0], dev("y", 0)).wait_send()

    return (msgs, end), result


REDUCE_MSGS = {("y", "z"): NY * NZ + NZ, ("z", "y"): NZ * NY + NY}


def greet(devices):
    barrier = pltpu.get_barrier_semaphore()
    for dev in devices:
        pl.semaphore_signal(barrier, inc=1, device_id=dev, device_id_type=MESH)
    pl.semaphore_wait(barrier, len(devices))


def nt(a, b):
    return lax.dot_general(a, b, (((1,), (1,)), ((), ())), preferred_element_type=F32)


def tn(a, b):
    return lax.dot_general(a, b, (((0,), (0,)), ((), ())), preferred_element_type=F32)


def nn(a, b):
    return lax.dot_general(a, b, (((1,), (0,)), ((), ())), preferred_element_type=F32)


def kernel_a(
    rand_any, glob_any, q_any, k, v, d_any,
    att, dq, contrib, dense, near_sum, gout, rand_sib,
    col_k, col_v, gown, g_got, g_out_buf, sel, xm_a, xm_b, xm_c, xm_d, xs, xall, stat, part,
    rand, glob, q, d, sg, dpg, gp, gs, gq, gd, kc, vc, qs, ds_, dkv, own_sum,
    a_ssem, a_rsem, b_ssem, b_rsem, g_ssem, g_rsem, c_ssem, c_rsem, x_ssem, x_rsem, ssem, rsem, lsem,
):
    x, y, z, c = here()
    col, xm = (col_k, col_v), ((xm_a, xm_b), (xm_c, xm_d))
    pb, ka = lax.axis_index("pb"), lax.axis_index("ka")
    shard = pb * 8 + ka
    me = y * NZ + z
    row = c * 4 + x
    zh = z // 4
    pos = (x, y, z)

    def row_dev(r):
        return device(r % 4, y, z, r // 4)

    def x_dev(step):
        return device((x + step + 4) % 4, y, z, c)

    row_peers = [(row + i) % 8 for i in range(1, 8)]
    sibling = row_dev((row + 4) % 8)

    local = [
        pltpu.make_async_copy(k, col[0].at[c, me], lsem.at[0]),
        pltpu.make_async_copy(v, col[1].at[c, me], lsem.at[1]),
        pltpu.make_async_copy(q_any, q, lsem.at[2]),
        pltpu.make_async_copy(d_any, d, lsem.at[3]),
        pltpu.make_async_copy(rand_any, rand, lsem.at[4]),
        pltpu.make_async_copy(glob_any, glob, lsem.at[5]),
    ]
    for cp in local:
        cp.start()
    greet(
        [
            device(x, (y + 1) % NY, z, c), device(x, (y + NY - 1) % NY, z, c),
            device(x, y, (z + 1) % NZ, c), device(x, y, (z + NZ - 1) % NZ, c),
        ]
        + [row_dev(r) for r in row_peers]
    )
    for cp in local:
        cp.wait()
    rand_copy = remote(rand_any, rand_sib, ssem.at[2], rsem.at[2], sibling)
    rand_copy.start()

    def pass_on(kv):
        def arrived(py, pz):
            ref = col[kv].at[c, py * NZ + pz]
            remote(ref, ref, ssem.at[3 + kv], rsem.at[3 + kv], sibling).start()

        return arrived

    def piece(kv):
        return lambda py, pz: col[kv].at[c, py * NZ + pz]

    def half(kv):
        return lambda py, pz, h: col[kv].at[c, py * NZ + pz, h]

    def some(kv):
        return col[kv].at[0, pl.ds(0, PLANE - 1)]

    flow_k = gather_flow(
        piece(0), half(0), ("y", "z"), pos, c, (a_ssem, a_rsem), pass_on(0), 32, some(0)
    )
    flow_v = gather_flow(
        piece(1), half(1), ("z", "y"), pos, c, (b_ssem, b_rsem), pass_on(1), 32, some(1)
    )
    pass_on(0)(y, z)
    pass_on(1)(y, z)

    g_place = [place(glob[g]) for g in range(2)]
    shards = jnp.full((16, HD), shard, jnp.int32)
    for g in range(2):
        mine = shards == glob[g] // 2
        for t, ref in ((0, q), (1, d)):
            for p in range(PLANE):
                value = ref[g_place[g][3], p % 4, :, (p // 4) * HD : (p // 4 + 1) * HD]
                rows = slice((g * 2 + t) * 16, (g * 2 + t + 1) * 16)
                gown[p, rows, :] = jnp.where(mine, value, jnp.zeros_like(value))

    flow_g, tiles = reduce_flow(
        lambda py, pz: gown.at[py * NZ + pz], g_got, g_out_buf, ("y", "z"), pos, c, (g_ssem, g_rsem),
        None, 16,
    )

    for j in range(2):
        for h in range(HEADS):
            rows = pl.ds(j * 512 + h * 64, 64)
            qs[rows, :] = q[j, :, :, h * HD : (h + 1) * HD].reshape(64, HD)
            ds_[rows, :] = d[j, :, :, h * HD : (h + 1) * HD].reshape(64, HD)

    def send_sel():
        sel[row] = tiles().reshape(2, 2, 16, HD).astype(BF16)
        for r in row_peers:
            remote(sel.at[row], sel.at[row], ssem.at[6], rsem.at[6], row_dev(r)).start()

    def wait_sel():
        remote(sel.at[pl.ds(0, 7)], sel.at[pl.ds(0, 7)], ssem.at[6], rsem.at[6], sibling).wait_recv()

    def wanted(ka_of, slot):
        if slot >= 6:
            return glob[slot - 6]
        return rand[slot % 3, ka_of * 2 + slot // 3]

    def ka_at(step):
        return zh * 4 + (x + step + 4) % 4

    def slot_at(direction, i):
        return i if direction == 0 else (i + 4) % 8

    def block_of(kv, block):
        bx, bc, bp, bh = place(block)
        return col[kv][bc, bp, bh]

    def x_copy(kv, dr, kind):
        src, dst = (
            (xs.at[kv, dr, pl.ds(9, 4)], xm[kv][dr].at[0]),
            (xs.at[kv, dr, pl.ds(4, 5)], xall.at[kv, dr, pl.ds(4, 5)]),
            (xs.at[kv, dr, pl.ds(0, 4)], xall.at[kv, dr, pl.ds(0, 4)]),
        )[kind]
        sem = kv * 6 + dr * 3 + kind
        return remote(src, dst, x_ssem.at[sem], x_rsem.at[sem], x_dev(1 - 2 * dr))

    def column_in(kv):
        ref = col[kv].at[1 - c]
        remote(ref, ref, ssem.at[3 + kv], rsem.at[3 + kv], sibling).wait_recv()

    def send_far(kv, dr):
        for i in range(4):
            xs[kv, dr, 9 + i] = block_of(kv, wanted(ka_at(2), slot_at(dr, i)))
        x_copy(kv, dr, 0).start()

    def send_near(kv, dr):
        step = 1 - 2 * dr
        for i in range(4, 8):
            xs[kv, dr, i] = block_of(kv, wanted(ka_at(step), slot_at(dr, i)))
        to = pb * 8 + ka_at(step)
        edge = (to * 2 + 2 * SHARDS - 1) % NBLK if dr == 0 else (to * 2 + 2) % NBLK
        xs[kv, dr, 8] = block_of(kv, edge)
        x_copy(kv, dr, 1).start()
        for i in range(4):
            xm[kv][dr][1, i] = block_of(kv, wanted(ka_at(step), slot_at(dr, i)))
        for i in range(4):
            xall[kv, 2, dr * 4 + i] = block_of(kv, wanted(ka, dr * 4 + i))

    def send_merged(kv, dr):
        for i in range(4):
            bx = place(wanted(ka_at(1 - 2 * dr), slot_at(dr, i)))[0]
            xs[kv, dr, i] = xm[kv][dr][jnp.where(bx == x, 1, 0), i]
        x_copy(kv, dr, 2).start()

    def global_scores():
        for g in range(2):
            gx, gc, gpl, gh = g_place[g]
            gq[pl.ds(g * 16, 16), :] = sel[gc * 4 + gx, g, 0]
            gd[pl.ds(g * 16, 16), :] = sel[gc * 4 + gx, g, 1]
        for i in range(4):
            lanes, ps = slice(i * 1024, (i + 1) * 1024), pl.ds(i * 8, 8)
            sg[:, lanes] = nt(gq[...], col[0][c, ps].reshape(1024, HD)) * SCALE
            dpg[:, lanes] = nt(gd[...], col[1][c, ps].reshape(1024, HD))
        g_max = jnp.max(sg[...], axis=1, keepdims=True)
        g_exp = jnp.exp(sg[...] - g_max)
        g_sum = jnp.sum(g_exp, axis=1, keepdims=True)
        g_dot = jnp.sum(g_exp * dpg[...], axis=1, keepdims=True)
        lane = lax.broadcasted_iota(jnp.int32, (32, HD), 1)
        stat[row] = jnp.where(lane == 0, g_max, jnp.where(lane == 1, g_sum, g_dot))
        for r in row_peers:
            remote(stat.at[row], stat.at[row], ssem.at[8], rsem.at[8], row_dev(r)).start()

    nothing = lambda: None

    def exchange(members):
        keys, values, rows_g = members
        n = len(keys) + len(values) + len(rows_g)
        more = [(rows_g, None, 2.5, 0.1, send_sel, wait_sel)]
        for kv, flow in ((0, keys), (1, values)):
            here_in = n + len(more)
            more.append((flow, None, 1.6, 0.0, nothing, lambda kv=kv: column_in(kv)))
            far = n + len(more)
            for kind, send, deps, kb in (
                (0, send_far, lambda dr: [here_in], 64),
                (1, send_near, lambda dr: [here_in], 80),
                (2, send_merged, lambda dr: [here_in, far + dr, far + 2 + dr], 64),
            ):
                for dr in range(2):
                    more.append(
                        (
                            deps(dr), ("x", dr), kb, 0.2,
                            lambda kv=kv, dr=dr, send=send: send(kv, dr),
                            lambda kv=kv, dr=dr, kind=kind: x_copy(kv, dr, kind).wait_recv(),
                        )
                    )
        more.append((keys + values + [n], None, 0.1, 1.5, global_scores, nothing))
        return more

    play((flow_k, flow_v, flow_g), exchange, favour=0)

    slot_of = lax.broadcasted_iota(jnp.int32, (1, 512), 1) // BLOCK
    for j in range(2):
        block = shard * 2 + j
        cand = [block - 1, block, block + 1, glob[0], glob[1]]
        cand += [rand[r, ka * 2 + j] for r in range(3)]
        for kv, dst in ((0, kc), (1, vc)):
            near_refs = [xall.at[kv, 0, 8], col[kv].at[c, me, 0], col[kv].at[c, me, 1], xall.at[kv, 1, 8]]
            for i in range(3):
                dst[i * BLOCK : (i + 1) * BLOCK, :] = near_refs[i + j][...]
            for i in range(3, 8):
                slot = 6 + i - 3 if i < 5 else j * 3 + i - 5
                far = 0 if slot < 4 else 1
                off = (place(cand[i])[0] + 4 - x) % 4
                src = jnp.where(off == 0, 2, jnp.where(off == 3, 0, jnp.where(off == 1, 1, far)))
                spot = jnp.where(src == 1, (slot + 4) % 8, slot)
                dst[i * BLOCK : (i + 1) * BLOCK, :] = xall[kv, src, spot]
        cands = jnp.zeros((1, 512), jnp.int32)
        for i in range(8):
            cands = jnp.where(slot_of == i, cand[i], cands)
        out = (cands < 0) | (cands >= NBLK)
        for i in range(7):
            out = out | ((slot_of > i) & (cands == cand[i]))
        bias = jnp.where(out, NEG, 0.0)
        blocks = jnp.full((256, 1), block, jnp.int32)
        keep = jnp.where((blocks == glob[0]) | (blocks == glob[1]), 0.0, 1.0)
        for part_i in range(2):
            rows = pl.ds(j * 512 + part_i * 256, 256)
            qv, dv = qs[rows, :], ds_[rows, :]
            s = nt(qv, kc[...]) * SCALE + bias
            e = jnp.exp(s - jnp.max(s, axis=1, keepdims=True))
            w = e * (keep / jnp.sum(e, axis=1, keepdims=True))
            wb = w.astype(BF16)
            o = nn(wb, vc[...]).astype(BF16)
            dot = jnp.sum(dv.astype(F32) * o.astype(F32), axis=1, keepdims=True)
            ds = (w * (nt(dv, vc[...]) - dot)).astype(BF16)
            dqv = (nn(ds, kc[...]) * SCALE).astype(BF16)
            for h in range(4):
                cols = slice((part_i * 4 + h) * HD, (part_i * 4 + h + 1) * HD)
                att[j, :, :, cols] = o[h * 64 : (h + 1) * 64].reshape(4, 16, HD)
                dq[j, :, :, cols] = dqv[h * 64 : (h + 1) * 64].reshape(4, 16, HD)
            dk_new, dv_new = tn(ds, qv) * SCALE, tn(wb, dv)
            if part_i == 0:
                dkv[0], dkv[1] = dk_new, dv_new
            else:
                dkv[0] += dk_new
                dkv[1] += dv_new
        for kv in range(2):
            for i in range(8):
                term = dkv[kv, i * BLOCK : (i + 1) * BLOCK, :]
                spot = i + j - 1
                if i < 3 and spot in (-1, 2):
                    contrib[row, 9 if spot == -1 else 0, kv] = term.astype(BF16)
                elif i < 3:
                    if (j, i) in ((0, 1), (0, 2)):
                        own_sum[kv, pl.ds(spot * BLOCK, BLOCK), :] = term
                    else:
                        total = own_sum[kv, pl.ds(spot * BLOCK, BLOCK), :] + term
                        near_sum[kv, pl.ds(spot * BLOCK, BLOCK), :] = total
                elif i >= 5:
                    contrib[row, 1 + j * 3 + i - 5, kv] = term.astype(BF16)
                elif j == 0:
                    own_sum[2 + kv, pl.ds((i - 3) * BLOCK, BLOCK), :] = term
                else:
                    total = own_sum[2 + kv, pl.ds((i - 3) * BLOCK, BLOCK), :] + term
                    contrib[row, 7 + i - 3, kv] = total.astype(BF16)

    def c_copy(src, first, n, step, sem):
        ref = contrib.at[src, pl.ds(first, n)]
        dev = sibling if step is None else x_dev(step)
        return remote(ref, ref, c_ssem.at[sem], c_rsem.at[sem], dev)

    def at_x(o):
        return c * 4 + (x + o + 4) % 4

    c_sends = [c_copy(row, 0, 9, 1, 0), c_copy(row, 1, 9, -1, 1), c_copy(row, 1, 8, None, 4)]
    for cp in c_sends:
        cp.start()

    remote(stat.at[pl.ds(0, 7)], stat.at[pl.ds(0, 7)], ssem.at[8], rsem.at[8], sibling).wait_recv()
    stats = [stat[i] for i in range(8)]
    top = stats[0][:, 0:1]
    for i in range(1, 8):
        top = jnp.maximum(top, stats[i][:, 0:1])
    total, dot = jnp.zeros((32, 1), F32), jnp.zeros((32, 1), F32)
    for i in range(8):
        f = jnp.exp(stats[i][:, 0:1] - top)
        total += stats[i][:, 1:2] * f
        dot += stats[i][:, 2:3] * f
    g_row = lax.broadcasted_iota(jnp.int32, (32, 1), 0)
    g_one = jnp.full((32, 1), glob[1], jnp.int32)
    first = jnp.where((g_row >= 16) & (g_one == glob[0]), 0.0, 1.0)
    gw = jnp.exp(sg[...] - top) * (first / total)
    gp[...] = gw.astype(BF16)
    gs[...] = (gw * (dpg[...] - dot / total)).astype(BF16)
    g_o, g_dq = jnp.zeros((32, HD), F32), jnp.zeros((32, HD), F32)
    for i in range(4):
        lanes, ps = slice(i * 1024, (i + 1) * 1024), pl.ds(i * 8, 8)
        g_o += nn(gp[:, lanes], col[1][c, ps].reshape(1024, HD))
        g_dq += nn(gs[:, lanes], col[0][c, ps].reshape(1024, HD))
    part[row, 0] = g_o
    part[row, 1] = g_dq * SCALE
    for r in row_peers:
        remote(part.at[row], part.at[row], ssem.at[11], rsem.at[11], row_dev(r)).start()

    c_copy(at_x(-1), 0, 9, 1, 0).wait_recv()
    more = [c_copy(at_x(-1), 1, 4, 1, 2), c_copy(at_x(-1), 0, 9, None, 5)]
    for cp in more:
        cp.start()
    c_copy(at_x(1), 1, 9, -1, 1).wait_recv()
    more += [c_copy(at_x(1), 5, 4, -1, 3), c_copy(at_x(1), 1, 9, None, 6)]
    for cp in more[2:]:
        cp.start()
    c_sends += more

    for i in range(4):
        lanes, ps = slice(i * 1024, (i + 1) * 1024), pl.ds(i * 8, 8)
        dense[ps, 0] = (tn(gs[:, lanes], gq[...]) * SCALE).reshape(8, HD, HD)
        dense[ps, 1] = tn(gp[:, lanes], gd[...]).reshape(8, HD, HD)

    c_copy(at_x(2), 1, 4, 1, 2).wait_recv()
    c_copy(at_x(2), 5, 4, -1, 3).wait_recv()
    last = c_copy(at_x(2), 1, 8, None, 7)
    last.start()
    c_sends.append(last)

    remote(part.at[pl.ds(0, 7)], part.at[pl.ds(0, 7)], ssem.at[11], rsem.at[11], sibling).wait_recv()
    for t in range(2):
        acc = part[0, t]
        for i in range(1, 8):
            acc += part[i, t]
        for g in range(2):
            gout[t, g] = acc[g * 16 : (g + 1) * 16].astype(BF16)

    def at_other(o):
        return (1 - c) * 4 + (x + o + 4) % 4

    for sem, o, first, n in ((4, 0, 1, 8), (5, -1, 0, 9), (6, 1, 1, 9), (7, 2, 1, 8)):
        c_copy(at_other(o), first, n, None, sem).wait_recv()
    rand_copy.wait_recv()

    for cp in c_sends + [rand_copy]:
        cp.wait_send()
    for kv in range(2):
        remote(col[kv].at[c], col[kv].at[c], ssem.at[3 + kv], rsem.at[3 + kv], sibling).wait_send()
    for ref, sem in ((sel, 6), (stat, 8), (part, 11)):
        remote(ref.at[pl.ds(0, 7)], ref.at[pl.ds(0, 7)], ssem.at[sem], rsem.at[sem], sibling).wait_send()
    for kv in range(2):
        for dr in range(2):
            for kind in range(3):
                x_copy(kv, dr, kind).wait_send()


def kernel_b(rand_any, rand_sib, glob_any, contrib, dense, acc, rand, glob, sem):
    x, y, z, c = here()
    zh = z // 4
    del dense
    copies = [
        pltpu.make_async_copy(rand_any, rand, sem.at[0]),
        pltpu.make_async_copy(glob_any, glob, sem.at[1]),
    ]
    for cp in copies:
        cp.start()
    for cp in copies:
        cp.wait()

    def add(block, here_too, src, entry):
        bx, bc, bp, bh = place(block)

        @pl.when(here_too & (bx == x) & (bc == c))
        def _():
            rows = pl.ds(pl.multiple_of(bh * BLOCK, BLOCK), BLOCK)
            acc[bp, :, rows, :] += contrib[src, entry].astype(F32)

    for core in range(2):
        for xs in range(NX):
            src = core * 4 + xs
            shard = ((y * 4 + z % 4) * 2 + core) * 8 + zh * 4 + xs
            for slot in range(SLOTS):
                if slot >= 6:
                    block = glob[slot - 6]
                else:
                    r, s = (zh * 4 + xs) * 2 + slot // 3, slot % 3
                    block = jnp.where(c == core, rand[s, r], rand_sib[s, r])
                add(block, True, src, 1 + slot)
            after, before = shard * 2 + 2, shard * 2 - 1
            add(jnp.minimum(after, NBLK - 1), (after < NBLK) & ((xs - x + 4) % 4 == 3), src, 0)
            add(jnp.maximum(before, 0), (before >= 0) & ((xs - x + 4) % 4 == 1), src, 9)


def kernel_c(
    acc, gout,
    sums, gall,
    got_k, out_k, got_v, out_v,
    k_ssem, k_rsem, v_ssem, v_rsem, o_ssem, o_rsem, w_ssem, w_rsem, lsem,
):
    x, y, z, c = here()
    me = y * NZ + z
    own = pltpu.make_async_copy(gout, gall.at[me], lsem.at[0])
    own.start()
    greet(
        [
            device(x, (y + 1) % NY, z, c), device(x, (y + NY - 1) % NY, z, c),
            device(x, y, (z + 1) % NZ, c), device(x, y, (z + NZ - 1) % NZ, c),
        ]
    )
    own.wait()
    pos = (x, y, z)

    def finish(kv):
        def done(value):
            sums[kv] = value

        return done

    def term(kv):
        return lambda py, pz: acc.at[py * NZ + pz, kv]

    def piece(t):
        return lambda py, pz: gall.at[py * NZ + pz, t]

    def half(t):
        return lambda py, pz, h: gall.at[py * NZ + pz, t, h]

    nothing = lambda py, pz: None
    some = [gall.at[pl.ds(0, PLANE - 1), t] for t in range(2)]
    play(
        (
            reduce_flow(term(0), got_k, out_k, ("z", "y"), pos, c, (k_ssem, k_rsem), finish(0), 32)[0],
            reduce_flow(term(1), got_v, out_v, ("y", "z"), pos, c, (v_ssem, v_rsem), finish(1), 32)[0],
            gather_flow(piece(0), half(0), ("y", "z"), pos, c, (o_ssem, o_rsem), nothing, 8, some[0]),
            gather_flow(piece(1), half(1), ("z", "y"), pos, c, (w_ssem, w_rsem), nothing, 8, some[1]),
        )
    )


def kernel_d(glob_any, sums, near_sum, att_in, dq_in, gall, att, dq, dk, dv, glob, sem):
    cp = pltpu.make_async_copy(glob_any, glob, sem.at[0])
    cp.start()
    shard = lax.axis_index("pb") * 8 + lax.axis_index("ka")
    dk[...] = (sums[0] + near_sum[0]).astype(BF16)
    dv[...] = (sums[1] + near_sum[1]).astype(BF16)
    cp.wait()
    for j in range(2):
        blocks = jnp.full((16, HD), shard * 2 + j, jnp.int32)
        is_glob = [blocks == glob[g] for g in range(2)]
        for t, src, dst in ((0, att_in, att), (1, dq_in, dq)):
            for p in range(PLANE):
                cols = slice((p // 4) * HD, (p // 4 + 1) * HD)
                value = jnp.where(is_glob[1], gall[p, t, 1], src[j, p % 4, :, cols])
                dst[j, p % 4, :, cols] = jnp.where(is_glob[0], gall[p, t, 0], value)


def in_hbm(value):
    return pltpu.with_memory_space_constraint(value, pltpu.HBM)


def body(queries, key_vectors, value_vectors, out_grad, rand_blocks, global_blocks):
    vmem = pl.BlockSpec(memory_space=pltpu.VMEM)
    smem = pl.BlockSpec(memory_space=pltpu.SMEM)
    hbm = pl.BlockSpec(memory_space=pl.ANY)
    off = pl.BlockSpec(memory_space=pltpu.HBM)
    shape = jax.ShapeDtypeStruct
    dma = pltpu.SemaphoreType.DMA
    rows = (2, 4, 16, HEADS * HD)
    rand = rand_blocks.T
    yz, zy = ("y", "z"), ("z", "y")
    ga, gb = GATHER_SEMS[yz], GATHER_SEMS[zy]
    mk, mv = REDUCE_MSGS[zy], REDUCE_MSGS[yz]
    att, dq, contrib, dense, near_sum, gout, rand_sib = pl.pallas_call(
        kernel_a,
        name="exchange_and_attend",
        out_shape=(
            shape(rows, BF16),
            shape(rows, BF16),
            shape((8, SLOTS + 2, 2, BLOCK, HD), BF16),
            shape((PLANE, 2, HD, HD), F32),
            shape((2, HD, HD), F32),
            shape((2, 2, 16, HD), BF16),
            shape((3, 16), jnp.int32),
        ),
        in_specs=[off] * 6,
        out_specs=(vmem, vmem, vmem, vmem, vmem, vmem, hbm),
        scratch_shapes=[
            pltpu.VMEM((2, PLANE, 2, BLOCK, HD), BF16),
            pltpu.VMEM((2, PLANE, 2, BLOCK, HD), BF16),
            pltpu.VMEM((PLANE, 64, HD), BF16),
            pltpu.VMEM((mv, 64, HD), BF16),
            pltpu.VMEM((mv, 64, HD), BF16),
            pltpu.VMEM((8, 2, 2, 16, HD), BF16),
            *[pltpu.VMEM((2, 4, BLOCK, HD), BF16)] * 4,
            pltpu.VMEM((2, 2, 13, BLOCK, HD), BF16),
            pltpu.VMEM((2, 3, 9, BLOCK, HD), BF16),
            pltpu.VMEM((8, 32, HD), F32),
            pltpu.VMEM((8, 2, 32, HD), F32),
            pltpu.SMEM((3, 16), jnp.int32),
            pltpu.SMEM((2,), jnp.int32),
            pltpu.VMEM(rows, BF16),
            pltpu.VMEM(rows, BF16),
            pltpu.VMEM((32, PLANE * HD), F32),
            pltpu.VMEM((32, PLANE * HD), F32),
            pltpu.VMEM((32, PLANE * HD), BF16),
            pltpu.VMEM((32, PLANE * HD), BF16),
            pltpu.VMEM((32, HD), BF16),
            pltpu.VMEM((32, HD), BF16),
            pltpu.VMEM((512, HD), BF16),
            pltpu.VMEM((512, HD), BF16),
            pltpu.VMEM((1024, HD), BF16),
            pltpu.VMEM((1024, HD), BF16),
            pltpu.VMEM((2, 512, HD), F32),
            pltpu.VMEM((4, HD, HD), F32),
            dma((1,)), dma((ga,)), dma((1,)), dma((gb,)), dma((1,)), dma((mv,)),
            dma((8,)), dma((8,)), dma((12,)), dma((12,)), dma((12,)), dma((12,)), dma((6,)),
        ],
        compiler_params=pltpu.CompilerParams(
            collective_id=0, has_side_effects=True, vmem_limit_bytes=VMEM_A
        ),
    )(
        *[
            in_hbm(value)
            for value in (
                rand, global_blocks, queries.reshape(rows), key_vectors.reshape(2, BLOCK, HD),
                value_vectors.reshape(2, BLOCK, HD), out_grad.reshape(rows),
            )
        ]
    )
    acc = pl.pallas_call(
        kernel_b,
        name="spread_terms",
        out_shape=shape((PLANE, 2, HD, HD), F32),
        in_specs=[off, smem, off, vmem, vmem],
        out_specs=vmem,
        scratch_shapes=[pltpu.SMEM((3, 16), jnp.int32), pltpu.SMEM((2,), jnp.int32), dma((2,))],
        input_output_aliases={4: 0},
        compiler_params=pltpu.CompilerParams(vmem_limit_bytes=VMEM_B),
    )(in_hbm(rand), rand_sib, in_hbm(global_blocks), contrib, dense)
    sums, gall = pl.pallas_call(
        kernel_c,
        name="reduce_and_gather",
        out_shape=(shape((2, HD, HD), F32), shape((PLANE, 2, 2, 16, HD), BF16)),
        in_specs=[vmem] * 2,
        out_specs=(vmem,) * 2,
        scratch_shapes=[
            pltpu.VMEM((mk, HD, HD), BF16), pltpu.VMEM((mk, HD, HD), BF16),
            pltpu.VMEM((mv, HD, HD), BF16), pltpu.VMEM((mv, HD, HD), BF16),
            dma((1,)), dma((mk,)), dma((1,)), dma((mv,)),
            dma((1,)), dma((ga,)), dma((1,)), dma((gb,)), dma((1,)),
        ],
        compiler_params=pltpu.CompilerParams(
            collective_id=1, has_side_effects=True, vmem_limit_bytes=VMEM_C
        ),
    )(acc, gout)
    att, dq, dk, dv = pl.pallas_call(
        kernel_d,
        name="finish",
        out_shape=(shape(rows, BF16), shape(rows, BF16), shape((HD, HD), BF16), shape((HD, HD), BF16)),
        in_specs=[off] + [vmem] * 5,
        out_specs=(vmem,) * 4,
        scratch_shapes=[pltpu.SMEM((2,), jnp.int32), dma((1,))],
        compiler_params=pltpu.CompilerParams(vmem_limit_bytes=VMEM_D),
    )(in_hbm(global_blocks), sums, near_sum, att, dq, gall)
    return att.reshape(queries.shape), dq.reshape(queries.shape), dk, dv


def solution(mesh):
    assert (mesh.shape["pb"], mesh.shape["ka"]) == (32, 8)
    rows = P(("pb", "ka"), None)
    return jax.shard_map(
        body,
        mesh=mesh,
        in_specs=(rows, rows, rows, rows, P("pb", None), P()),
        out_specs=(rows, rows, rows, rows),
        check_vma=False,
    )
```
